32 devices in a mesh: dp: 2 (over y), fsdp: 16 (over z, x, core).
Axes of the slice: x: 2, y: 2, z: 4, core: 2. Of those that a mesh axis runs over, the one named last changes fastest.
Arguments:
- tokens: bfloat16 [64, 512, 768], P(('dp', 'fsdp')), may hold values from -6 to 6
- out_grad: bfloat16 [64, 512, 768], P(('dp', 'fsdp')), may hold values from -6 to 6
- lengths: int32 [64], P(('dp', 'fsdp')), may hold values from 128 to 512, as said below
- labels: int32 [64], P(('dp', 'fsdp')), may hold values from 0 to 2
- exit_layers: int32 [64], P(('dp', 'fsdp')), may hold values from 0 to 11, as said below
- mat_master: float32 [9984, 768], P('fsdp')
- mat_first: float32 [9984, 768], P('fsdp')
- mat_second: float32 [9984, 768], P('fsdp'), as said below
- vec_master: float32 [16, 768], P(None, 'fsdp')
- vec_first: float32 [16, 768], P(None, 'fsdp')
- vec_second: float32 [16, 768], P(None, 'fsdp'), as said below
- cls_bias: float32 [3], replicated, may hold values from -3 to 3
- cls_first: float32 [3], replicated
- cls_second: float32 [3], replicated, as said below
Outputs:
- block_out: bfloat16 [64, 512, 768], P(('dp', 'fsdp'))
- input_grad: bfloat16 [64, 512, 768], P(('dp', 'fsdp'))
- ramp_loss: float32 [], replicated
- mat_master_new: float32 [9984, 768], P('fsdp')
- mat_first_new: float32 [9984, 768], P('fsdp')
- mat_second_new: float32 [9984, 768], P('fsdp')
- mat_copy: bfloat16 [9984, 768], P('fsdp')
- vec_master_new: float32 [16, 768], P(None, 'fsdp')
- vec_first_new: float32 [16, 768], P(None, 'fsdp')
- vec_second_new: float32 [16, 768], P(None, 'fsdp')
- vec_copy: bfloat16 [16, 768], P(None, 'fsdp')
- cls_bias_new: float32 [3], replicated
- cls_first_new: float32 [3], replicated
- cls_second_new: float32 [3], replicated
The draws below stay inside these ranges and needn't reach their ends.
Inputs may be any that keep to these rules, and one draw needn't show every extreme that they name: Keys at positions of lengths or later are padding; some sequence has 512 tokens and some 512 // 4. `exit_layers`: a sequence whose exit layer is below 6 has left the encoder and is out of the loss; some sequence exits at layer 0 and some at the last. `mat_second`: positive. `vec_second`: positive. `cls_second`: positive.
All inputs are finite; a program needn't handle non-finite values.
Results may differ from the reference program's by a relative error of at most 0.02.
Values may be sent and summed in bfloat16 or wider, within the bound.
No kernel may reach another device: no remote copies, remote signals or barrier semaphores. Data moves between devices by JAX's collectives and lax.ppermute only.
A program may use at most 192 MiB of HBM per device.

```python
import math
import jax
import jax.numpy as jnp
from jax import lax

D = 768
H = 12
HD = 64
FF = 3072
NLAYERS = 12
LAYER = 6
NCLS = 3
L = 512
STEP = 10
SEQS = 64
MROWS = 9984
VROWS = 16


def matrix_init_scale(row_index):
    base_scale = D ** (-0.5)
    return jnp.where((row_index >= 3 * D) & (row_index < 4 * D), 8.0 * base_scale, jnp.where(row_index >= 5 * D + FF, 1.5 * FF ** (-0.5), base_scale))


def matrix_grad_scale(row_index):
    root_tokens = (SEQS * L) ** 0.5
    ramp_scale = 0.3 * (2.0 / SEQS) ** 0.5
    return jnp.where(row_index < 3 * D, 0.5 * root_tokens, jnp.where(row_index < 4 * D, 0.15 * root_tokens, jnp.where(row_index < 5 * D, ramp_scale, jnp.where(row_index < 5 * D + FF, 0.3 * root_tokens, 0.35 * root_tokens))))


def vector_grad_scale(row_index):
    root_tokens = (SEQS * L) ** 0.5
    ramp_scale = 0.3 * (2.0 / SEQS) ** 0.5
    inner_rows = FF // D
    table = jnp.array([0.5, 0.5, 0.7, 1.0, 1.0, 0.7, 1.0, 1.0], jnp.float32)
    head_part = table[jnp.minimum(row_index, 7)] * root_tokens
    return jnp.where(row_index < 8, head_part, jnp.where(row_index == 8, ramp_scale, jnp.where(row_index < 9 + inner_rows, 0.26 * root_tokens, 0.8 * ramp_scale)))


def draw_lengths(key, part):
    base_draw = jax.random.randint(jax.random.fold_in(key, 11), (SEQS,), L // 4, L + 1)
    order = jax.random.permutation(jax.random.fold_in(key, 12), SEQS)
    base_draw = jnp.where(order == 0, L, base_draw)
    return jnp.where(order == 1, L // 4, base_draw).astype(jnp.int32)


def draw_exit_layers(key, part):
    base_draw = jax.random.randint(jax.random.fold_in(key, 21), (SEQS,), 0, NLAYERS)
    order = jax.random.permutation(jax.random.fold_in(key, 22), SEQS)
    base_draw = jnp.where(order == 0, NLAYERS - 1, base_draw)
    return jnp.where(order == 1, 0, base_draw).astype(jnp.int32)


def draw_mat_master(key, part):
    row_index = jnp.arange(MROWS)
    noise = jax.random.normal(jax.random.fold_in(key, 31), (MROWS, D), jnp.float32)
    return noise * matrix_init_scale(row_index)[:, None]


def draw_mat_first(key, part):
    row_index = jnp.arange(MROWS)
    noise = jnp.clip(jax.random.normal(jax.random.fold_in(key, 32), (MROWS, D), jnp.float32), -3.0, 3.0)
    return noise * (0.1 / 0.9) * matrix_grad_scale(row_index)[:, None]


def draw_mat_second(key, part):
    row_index = jnp.arange(MROWS)
    grad_size = matrix_grad_scale(row_index)[:, None]
    factor = jax.random.uniform(jax.random.fold_in(key, 33), (MROWS, D), jnp.float32, 1.0, 4.0)
    return factor * (0.001 / 0.999) * grad_size * grad_size


def draw_vec_master(key, part):
    row_index = jnp.arange(VROWS)[:, None]
    noise = jax.random.normal(jax.random.fold_in(key, 41), (VROWS, D), jnp.float32)
    gains = 1.0 + jax.random.uniform(jax.random.fold_in(key, 42), (VROWS, D), jnp.float32, -0.3, 0.3)
    class_rows = row_index >= 9 + FF // D
    gain_rows = (row_index == 3) | (row_index == 6)
    return jnp.where(gain_rows, gains, jnp.where(class_rows, noise * 3.0 * D ** (-0.5), noise * 0.3))


def draw_vec_first(key, part):
    row_index = jnp.arange(VROWS)
    noise = jnp.clip(jax.random.normal(jax.random.fold_in(key, 43), (VROWS, D), jnp.float32), -3.0, 3.0)
    return noise * (0.1 / 0.9) * vector_grad_scale(row_index)[:, None]


def draw_vec_second(key, part):
    row_index = jnp.arange(VROWS)
    grad_size = vector_grad_scale(row_index)[:, None]
    factor = jax.random.uniform(jax.random.fold_in(key, 44), (VROWS, D), jnp.float32, 1.0, 4.0)
    return factor * (0.001 / 0.999) * grad_size * grad_size


def draw_cls_first(key, part):
    grad_size = 0.5 * (2.0 / SEQS) ** 0.5
    noise = jnp.clip(jax.random.normal(jax.random.fold_in(key, 51), (NCLS,), jnp.float32), -3.0, 3.0)
    return noise * (0.1 / 0.9) * grad_size


def draw_cls_second(key, part):
    grad_size = 0.5 * (2.0 / SEQS) ** 0.5
    factor = jax.random.uniform(jax.random.fold_in(key, 52), (NCLS,), jnp.float32, 1.0, 4.0)
    return factor * (0.001 / 0.999) * grad_size * grad_size


def touch_ends(drawn, rng, smallest, high):
    spot = [jax.random.randint(jax.random.fold_in(rng, axis), (), 0, length) for axis, length in enumerate(drawn.shape)]
    widest = drawn.shape.index(max(drawn.shape))
    beside = spot[:widest] + [(spot[widest] + 1) % drawn.shape[widest]] + spot[widest + 1:]
    return drawn.at[tuple(spot)].set(smallest).at[tuple(beside)].set(high)


def steps_of(key, extent, cuts, smallest, top_value):
    level = 1.0
    for position, shards_of in cuts:
        heights = jax.random.uniform(jax.random.fold_in(jax.random.fold_in(key, 6), position), (shards_of,), jnp.float32, smallest / len(cuts), top_value / len(cuts))
        level = level * jnp.repeat(jnp.exp(heights), extent[position] // shards_of).reshape((-1,) + (1,) * (len(extent) - 1 - position))
    return level


def scatter_about(rng, dims, width, bound, cuts=(), dtype=jnp.bfloat16):
    level = steps_of(rng, dims, cuts, -0.22, 0.18) if cuts else 1.0
    drawn = jax.random.normal(rng, dims, jnp.float32) * width * level
    return jnp.minimum(jnp.maximum(drawn, -bound), bound).astype(dtype)


def setup_inputs(seed: int = 0) -> dict:
    keys = jax.random.split(jax.random.key(seed), 15)
    return {
        "tokens": scatter_about(keys[0], (SEQS, L, D), 1.0, 6.0, ((0, 32),)),
        "out_grad": scatter_about(keys[1], (SEQS, L, D), 1.0, 6.0, ((0, 32),)),
        "lengths": draw_lengths(jax.random.fold_in(keys[14], 71), 0),
        "labels": touch_ends(jax.random.randint(keys[3], (SEQS,), 0, NCLS), jax.random.fold_in(keys[3], 1), 0, NCLS - 1).astype(jnp.int32),
        "exit_layers": draw_exit_layers(jax.random.fold_in(keys[14], 71), 0),
        "mat_master": draw_mat_master(jax.random.fold_in(keys[14], 71), 0),
        "mat_first": draw_mat_first(jax.random.fold_in(keys[14], 71), 0),
        "mat_second": draw_mat_second(jax.random.fold_in(keys[14], 71), 0),
        "vec_master": draw_vec_master(jax.random.fold_in(keys[14], 71), 0),
        "vec_first": draw_vec_first(jax.random.fold_in(keys[14], 71), 0),
        "vec_second": draw_vec_second(jax.random.fold_in(keys[14], 71), 0),
        "cls_bias": scatter_about(keys[11], (NCLS,), 0.5, 3.0, (), jnp.float32),
        "cls_first": draw_cls_first(jax.random.fold_in(keys[14], 71), 0),
        "cls_second": draw_cls_second(jax.random.fold_in(keys[14], 71), 0),
    }


@jax.custom_vjp
def low(v):
    return lax.optimization_barrier(v.astype(jnp.bfloat16)).astype(jnp.float32)

@jax.custom_vjp
def low_back(v):
    return v

def low_keep(v):
    return (low(v), None)

def low_pass(kept, grad):
    return (grad,)

def back_keep(v):
    return (v, None)

def back_low(kept, grad):
    return (low(grad),)
low.defvjp(low_keep, low_pass)
low_back.defvjp(back_keep, back_low)
HIGHEST = lax.Precision.HIGHEST
BETA_ONE = 0.9
BETA_TWO = 0.999
ADAM_EPS = 1e-08
WEIGHT_DECAY = 0.01
LN_EPS = 1e-12
VEC_RATE = 0.5
MASK_FILL = -1000000000.0

def matmul(first_arg, second_arg):
    return jnp.dot(first_arg, second_arg, precision=HIGHEST, preferred_element_type=jnp.float32)

def layer_norm(hidden, gain_vec, shift_vec):
    centre = lax.optimization_barrier(jnp.mean(hidden, axis=-1, keepdims=True))
    centred = hidden - centre
    spread = lax.optimization_barrier(jnp.mean(centred * centred, axis=-1, keepdims=True))
    return centred * lax.rsqrt(spread + LN_EPS) * gain_vec + shift_vec

def split_matrices(matrices):
    return (matrices[0:D], matrices[D:2 * D], matrices[2 * D:3 * D], matrices[3 * D:4 * D], matrices[4 * D:5 * D], matrices[5 * D:5 * D + FF], matrices[5 * D + FF:5 * D + 2 * FF])

def split_vectors(vectors):
    inner_rows = FF // D
    return (vectors[0], vectors[1], vectors[2], vectors[3], vectors[4], vectors[5], vectors[6], vectors[7], vectors[8], vectors[9:9 + inner_rows].reshape(FF), vectors[9 + inner_rows:9 + inner_rows + NCLS])

def row_rates(row_index):
    base_rate = D ** (-0.5)
    return jnp.where((row_index >= 3 * D) & (row_index < 4 * D), 8.0 * base_rate, jnp.where(row_index >= 5 * D + FF, 1.5 * FF ** (-0.5), base_rate))

def adam_update(master, first_mom, second_mom, grad_in, rate, decay):
    first_new = BETA_ONE * first_mom + (1.0 - BETA_ONE) * grad_in
    second_new = BETA_TWO * second_mom + (1.0 - BETA_TWO) * grad_in * grad_in
    fix_one = 1.0 - BETA_ONE ** STEP
    fix_two = 1.0 - BETA_TWO ** STEP
    direction = first_new / fix_one / (jnp.sqrt(second_new / fix_two) + ADAM_EPS)
    master_new = master - rate * (direction + decay * master)
    return (master_new, first_new, second_new)

def block_forward(token_block, matrices, vectors, class_bias, length_block, label_block, active_block, active_count):
    group_size = token_block.shape[0]
    w_query, w_key, w_value, w_out, w_pool, w_inner, w_outer = split_matrices(matrices)
    b_query, b_value, b_out, gain_one, shift_one, b_outer, gain_two, shift_two, b_pool, b_inner, w_class = split_vectors(vectors)
    token_rows = token_block.reshape(group_size * L, D)
    query_rows = low(low_back(matmul(token_rows, w_query) + b_query))
    key_rows = low(low_back(matmul(token_rows, w_key)))
    value_rows = low(low_back(matmul(token_rows, w_value) + b_value))
    q_heads = query_rows.reshape(group_size, L, H, HD)
    k_heads = key_rows.reshape(group_size, L, H, HD)
    v_heads = value_rows.reshape(group_size, L, H, HD)
    scores = low_back(jnp.einsum('bqhd,bkhd->bhqk', q_heads, k_heads, precision=HIGHEST) * HD ** (-0.5))
    key_valid = jnp.arange(L)[None, :] < length_block[:, None]
    scores = jnp.where(key_valid[:, None, None, :], scores, MASK_FILL)
    attn_probs = low(jax.nn.softmax(scores, axis=-1))
    context = jnp.einsum('bhqk,bkhd->bqhd', attn_probs, v_heads, precision=HIGHEST)
    context = low(low_back(context.reshape(group_size * L, D)))
    attn_out = low_back(matmul(context, w_out) + b_out)
    normed_one = layer_norm(token_rows + attn_out, gain_one, shift_one)
    inner_pre = low_back(matmul(low(normed_one), w_inner.T) + b_inner)
    activated = low(jax.nn.gelu(inner_pre, approximate=False))
    ffn_out = low_back(matmul(activated, w_outer) + b_outer)
    layer_out = layer_norm(normed_one + ffn_out, gain_two, shift_two)
    layer_out = layer_out.reshape(group_size, L, D)
    first_row = low(layer_out[:, 0, :])
    pooled = jnp.tanh(low_back(matmul(first_row, w_pool) + b_pool))
    logits = low_back(matmul(low(pooled), w_class.T)) + class_bias
    onehot = (label_block[:, None] == jnp.arange(NCLS)[None, :]).astype(jnp.float32)
    cross_ent = jax.nn.logsumexp(logits, axis=-1) - lax.optimization_barrier(jnp.sum(logits * onehot, axis=-1))
    loss_part = jnp.sum(active_block * cross_ent) / active_count
    return (layer_out, loss_part)

def reference(tokens, out_grad, lengths, labels, exit_layers, mat_master, mat_first, mat_second, vec_master, vec_first, vec_second, cls_bias, cls_first, cls_second):
    matrices = low(mat_master)
    vectors = low(vec_master)
    active = (exit_layers >= LAYER).astype(jnp.float32)
    active_count = jnp.sum(active)
    group_size = math.gcd(SEQS, max(1, 4096 // L))
    group_count = SEQS // group_size
    items = (tokens.reshape(group_count, group_size, L, D), out_grad.reshape(group_count, group_size, L, D), lengths.reshape(group_count, group_size), labels.reshape(group_count, group_size), active.reshape(group_count, group_size))

    def one_group(carry, item_parts):
        token_block, grad_block, length_block, label_block, active_block = item_parts

        def forward(token_f, mat_f, vec_f, bias_f):
            return block_forward(token_f, mat_f, vec_f, bias_f, length_block, label_block, active_block, active_count)
        (layer_out, loss_part), pullback = jax.vjp(forward, token_block.astype(jnp.float32), matrices, vectors, cls_bias)
        grad_tok, grad_mat, grad_vec, grad_cls = pullback((grad_block.astype(jnp.float32), jnp.ones((), jnp.float32)))
        new_carry = (carry[0] + grad_mat, carry[1] + grad_vec, carry[2] + grad_cls, carry[3] + loss_part)
        return (new_carry, (layer_out.astype(jnp.bfloat16), grad_tok.astype(jnp.bfloat16)))
    start = (jnp.zeros((MROWS, D), jnp.float32), jnp.zeros((VROWS, D), jnp.float32), jnp.zeros((NCLS,), jnp.float32), jnp.zeros((), jnp.float32))
    totals, outs_all = lax.scan(one_group, start, items)
    mat_grad, vec_grad, cls_grad, ramp_loss = totals
    block_out = outs_all[0].reshape(SEQS, L, D)
    input_grad = outs_all[1].reshape(SEQS, L, D)
    rates = row_rates(jnp.arange(MROWS))[:, None]
    mat_new, mat_first_new, mat_second_new = adam_update(mat_master, mat_first, mat_second, mat_grad, rates, WEIGHT_DECAY)
    vec_new, vec_first_new, vec_second_new = adam_update(vec_master, vec_first, vec_second, vec_grad, VEC_RATE, 0.0)
    cls_new, cls_first_new, cls_second_new = adam_update(cls_bias, cls_first, cls_second, cls_grad, VEC_RATE, 0.0)
    return (block_out, input_grad, ramp_loss, mat_new, mat_first_new, mat_second_new, mat_new.astype(jnp.bfloat16), vec_new, vec_first_new, vec_second_new, vec_new.astype(jnp.bfloat16), cls_new, cls_first_new, cls_second_new)
```

```python
import functools
import math

import jax
import jax.numpy as jnp
from jax import lax
from jax.experimental import pallas as pl
from jax.experimental.pallas import tpu as pltpu
from jax.sharding import PartitionSpec as P

D, H, HD, FF, NCLS, L = 768, 12, 64, 3072, 3, 512
LAYER = 6
STEP = 10
BETA_ONE = 0.9
BETA_TWO = 0.999
ADAM_EPS = 1e-08
WEIGHT_DECAY = 0.01
VEC_RATE = 0.5
LN_EPS = 1e-12
MASK_FILL = -1e9
LOG2E = 1.4426950408889634
f32, bf16 = jnp.float32, jnp.bfloat16
NN = (((1,), (0,)), ((), ()))
NT = (((1,), (1,)), ((), ()))
TN = (((0,), (0,)), ((), ()))
def dot(a, b, dims=NN):
    return lax.dot_general(a, b, dims, preferred_element_type=f32)
ANY = pl.BlockSpec(memory_space=pl.ANY)
HBM = pl.BlockSpec(memory_space=pltpu.HBM)
MROWS = 5 * D + 2 * FF
SMEM = pl.BlockSpec(memory_space=pltpu.SMEM)
TILE = 256
R = 16
ERF_P = 0.3275911
ERF_A = (0.254829592, -0.284496736, 1.421413741, -1.453152027, 1.061405429)

class Loads:
    def __init__(self, plan, refs, place, dst, sems, low, high):
        self.items = []
        for j, (piece, src, count, row) in enumerate(plan.spans):
            if isinstance(row, int):
                first, last = max(row, low), min(row + count, high)
                if first >= last:
                    continue
                cond = None
                source = refs[piece].at[pl.ds(src + first - row, last - first)]
                target = dst.at[pl.ds(first - low, last - first)]
            else:
                shard, at = plan.locate(row, place)
                cond = (shard * plan.rows >= low) & (shard * plan.rows < high)
                source = refs[piece].at[pl.ds(plan.skip(src, row, place), count)]
                target = dst.at[pl.ds(pl.multiple_of(jnp.where(cond, at - low, 0), 16), count)]
            self.items.append((cond, pltpu.make_async_copy(source, target, sems.at[j])))

    def start(self):
        for cond, copy in self.items:
            if cond is None:
                copy.start()
            else:
                pl.when(cond)(copy.start)

    def wait(self):
        for cond, copy in self.items:
            if cond is None:
                copy.wait()
            else:
                pl.when(cond)(copy.wait)


class Plan:
    def __init__(self, spans, rows, first=0):
        self.spans, self.rows, self.first = spans, rows, first
        self.part_e = -(-(rows // 2 - first) // 16) * 16
        self.head_end = -(-3 * D // rows) * rows
        self.tail_start = 3 * D // rows * rows

    def locate(self, where, place):
        steps, other_x, other_core, part = where
        z, x, core, rep = (place[i] for i in range(4))
        flip = lambda bit, other: 1 - bit if other else bit
        shard = (lax.rem(z - steps + 4, 4) * 2 + flip(x, other_x)) * 2 + flip(core, other_core)
        low_e = 2 * self.first
        part_e, size_e = self.part_e, self.rows - low_e
        base = {
            "all": 0,
            "e": low_e,
            "c_mine": rep * self.first,
            "c_other": (1 - rep) * self.first,
            "e_mine": low_e + rep * (size_e - part_e),
            "e_other": low_e + (1 - rep) * part_e,
        }[part]
        return shard, shard * self.rows + base

    def skip(self, start, where, place):
        if where[3] != "e_other":
            return start
        return pl.multiple_of(start + (1 - place[3]) * (2 * (self.first + self.part_e) - self.rows), 16)


def attn_fwd_kernel(plan, n, place, lens, x_ref, vec_ref, *refs):
    pieces = refs[:n]; qkv_ref, ctx_ref, st_ref, w, sems = refs[n:]
    s = pl.program_id(0)
    @pl.when(s == 0)
    def _():
        ld = Loads(plan, pieces, place, w, sems, 0, plan.head_end)
        ld.start(); ld.wait()
    x = x_ref[0]
    for i, b in ((0, 0), (1, None), (2, 1)):
        r = dot(x, w[i * D:(i + 1) * D])
        if b is not None: r = r + vec_ref[b:b + 1]
        qkv_ref[0, :, i * D:(i + 1) * D] = r.astype(bf16)
    length = lens[s]
    lane = lax.broadcasted_iota(jnp.int32, (L, 128), 1)
    low = lane < HD
    valid = lax.broadcasted_iota(jnp.int32, (1, L), 1) < length
    ones = jnp.ones((L, 128), bf16)
    stats = jnp.zeros((L, 128), f32)
    scale = LOG2E * HD ** -0.5
    for p in range(H // 2):
        q2 = qkv_ref[0, :, p * 128:(p + 1) * 128]
        k2 = qkv_ref[0, :, D + p * 128:D + (p + 1) * 128]
        v2 = qkv_ref[0, :, 2 * D + p * 128:2 * D + (p + 1) * 128]
        va = jnp.concatenate([v2, ones], axis=1)
        outs = []
        for h in range(2):
            qm = jnp.where(low if h == 0 else ~low, q2, jnp.zeros_like(q2))
            sc = jnp.where(valid, dot(qm, k2, NT) * scale, MASK_FILL)
            top = jnp.max(sc, axis=1, keepdims=True)
            e = jnp.exp2(sc - top).astype(bf16)
            o = dot(e, va)
            tot = o[:, 128:]
            outs.append(o[:, :128] / tot)
            stats = jnp.where(lane == 2 * p + h, top + jnp.log2(tot), stats)
        ctx_ref[0, :, p * 128:(p + 1) * 128] = jnp.where(low, outs[0], outs[1]).astype(bf16)
    st_ref[0] = stats.T

def attn_fwd(plan, pieces, place, lengths, tokens, vec):
    n = len(pieces); S = tokens.shape[0]
    return pl.pallas_call(
        functools.partial(attn_fwd_kernel, plan, n), grid=(S,), name="attn_fwd",
        in_specs=[SMEM, SMEM, pl.BlockSpec((1, L, D), lambda s: (s, 0, 0)), pl.BlockSpec((16, D), lambda s: (0, 0))] + [HBM] * n,
        out_specs=[pl.BlockSpec((1, L, 3 * D), lambda s: (s, 0, 0)), pl.BlockSpec((1, L, D), lambda s: (s, 0, 0)), pl.BlockSpec((1, 128, L), lambda s: (s, 0, 0))],
        out_shape=[jax.ShapeDtypeStruct((S, L, 3 * D), bf16), jax.ShapeDtypeStruct((S, L, D), bf16), jax.ShapeDtypeStruct((S, 128, L), f32)],
        scratch_shapes=[pltpu.VMEM((plan.head_end, D), bf16), pltpu.SemaphoreType.DMA((len(plan.spans),))],
        compiler_params=pltpu.CompilerParams(vmem_limit_bytes=50 << 20),
        cost_estimate=pl.CostEstimate(flops=8 * 10 ** 9, bytes_accessed=14 * 10 ** 6, transcendentals=6 * 10 ** 6),
    )(place, lengths, tokens, vec, *pieces)

def norm(h):
    mu = jnp.mean(h, axis=1, keepdims=True)
    c = h - mu
    r = lax.rsqrt(jnp.mean(c * c, axis=1, keepdims=True) + LN_EPS)
    return c * r, r

def norm_back(g, xh, r, gain):
    a = g * gain
    return r * (a - jnp.mean(a, axis=1, keepdims=True) - xh * jnp.mean(a * xh, axis=1, keepdims=True))

def gelu_both(u):
    t = 1.0 / (1.0 + (ERF_P * 2 ** -0.5) * jnp.abs(u))
    bell = jnp.exp2(u * u * (-0.5 * LOG2E))
    a = [0.5 * v for v in ERF_A]
    poly = t * (a[0] + t * (a[1] + t * (a[2] + t * (a[3] + t * a[4]))))
    tail = poly * bell
    phi = jnp.where(u < 0, tail, 1.0 - tail)
    g = u * phi
    return g, phi + (u * bell) * (2 * math.pi) ** -0.5

def ffn_kernel(plan, n, tiles, low, place, labels, exits, count, cls, x_ref, c_ref, og_ref, vec_ref, *refs):
    pieces = refs[:n]
    out_ref, dh1_ref, dc_ref, vg_ref, sc_ref, gw_ref, w, sems, g_s, du_s, n1_s, df_s, da_s, cc_s, gp_s, dy_s, e_s, z_s, stage, osem = refs[n:]
    i = pl.program_id(0)
    ld = Loads(plan, pieces, place, w, sems, low, MROWS)
    @pl.when(i == 0)
    def _():
        ld.start()
        vg_ref[...] = jnp.zeros_like(vg_ref); sc_ref[...] = jnp.zeros_like(sc_ref)
        ld.wait()
    wo, wp, w1, w2 = 3 * D - low, 4 * D - low, 5 * D - low, 5 * D + FF - low
    vrow = lambda r: vec_ref[r:r + 1]
    rows = pl.ds(pl.multiple_of(i * TILE, TILE), TILE)
    c = c_ref[...]
    cc_s[rows] = c
    h1 = x_ref[...].astype(f32) + (dot(c, w[wo:wo + D]) + vrow(2))
    xh1, r1 = norm(h1)
    n1 = xh1 * vrow(3) + vrow(4)
    n1b = n1.astype(bf16)
    n1_s[rows] = n1b
    f = None
    for j in range(FF // D):
        u = dot(n1b, w[w1 + j * D:w1 + (j + 1) * D], NT) + vrow(9 + j)
        g, gp = gelu_both(u)
        gb = g.astype(bf16)
        g_s[rows, j * D:(j + 1) * D] = gb
        gp_s[:, j * D:(j + 1) * D] = gp
        part = dot(gb, w[w2 + j * D:w2 + (j + 1) * D])
        f = part if f is None else f + part
    xh2, r2 = norm(n1 + (f + vrow(5)))
    yb = (xh2 * vrow(6) + vrow(7)).astype(bf16)
    out_ref[...] = yb
    dy_s[...] = og_ref[...].astype(f32)
    per = L // TILE
    @pl.when(lax.rem(i, per) == 0)
    def _():
        s = i // per
        head = lax.broadcasted_iota(jnp.int32, (R, 1), 0) == 0
        act = jnp.where(head, jnp.where(exits[s] >= LAYER, 1.0, 0.0), 0.0)
        e8 = jnp.where(head, yb[:R].astype(f32), 0.0).astype(bf16)
        pool = jnp.tanh(dot(e8, w[wp:wp + D]) + vrow(8))
        pb = pool.astype(bf16).astype(f32)
        lg = [jnp.sum(pb * vrow(13 + k), axis=1, keepdims=True) + cls[k] for k in range(NCLS)]
        top = jnp.maximum(jnp.maximum(lg[0], lg[1]), lg[2])
        lse = top + jnp.log(jnp.exp(lg[0] - top) + jnp.exp(lg[1] - top) + jnp.exp(lg[2] - top))
        hot = [jnp.where(labels[s] == k, 1.0, 0.0) for k in range(NCLS)]
        ce = act * (lse - (lg[0] * hot[0] + lg[1] * hot[1] + lg[2] * hot[2]))
        err = [act * (jnp.exp(lg[k] - lse) - hot[k]) for k in range(NCLS)]
        lane = lax.broadcasted_iota(jnp.int32, (R, 128), 1)
        got = jnp.where(lane == 0, ce, 0.0)
        for k in range(NCLS): got = jnp.where(lane == 1 + k, err[k], got)
        sc_ref[...] += got
        dl = [(err[k] / count[0]).astype(bf16).astype(f32) for k in range(NCLS)]
        gpool = dl[0] * vrow(13) + dl[1] * vrow(14) + dl[2] * vrow(15)
        dz = (gpool * (1.0 - pool * pool)).astype(bf16)
        srow = pl.ds(pl.multiple_of(s * R, R), R)
        e_s[srow] = e8; z_s[srow] = dz
        vg_ref[8:9] += jnp.sum(dz.astype(f32), axis=0, keepdims=True)
        for k in range(NCLS): vg_ref[13 + k:14 + k] += jnp.sum(dl[k] * pb, axis=0, keepdims=True)
        dy_s[0:R] += dot(dz, w[wp:wp + D], NT)
    dy = dy_s[...]
    def vsum(r, v): vg_ref[r:r + 1] += jnp.sum(v, axis=0, keepdims=True)
    vsum(6, dy * xh2); vsum(7, dy)
    dh2 = norm_back(dy, xh2, r2, vrow(6))
    dfb = dh2.astype(bf16)
    df_s[rows] = dfb
    vsum(5, dfb.astype(f32))
    dn1 = dh2
    for j in range(FF // D):
        du = (dot(dfb, w[w2 + j * D:w2 + (j + 1) * D], NT) * gp_s[:, j * D:(j + 1) * D]).astype(bf16)
        du_s[rows, j * D:(j + 1) * D] = du
        vsum(9 + j, du.astype(f32))
        dn1 = dn1 + dot(du, w[w1 + j * D:w1 + (j + 1) * D])
    vsum(3, dn1 * xh1); vsum(4, dn1)
    dh1 = norm_back(dn1, xh1, r1, vrow(3))
    dh1_ref[...] = dh1
    dab = dh1.astype(bf16)
    da_s[rows] = dab
    vsum(2, dab.astype(f32))
    dc_ref[...] = dot(dab, w[wo:wo + D], NT).astype(bf16)
    @pl.when(i == tiles - 1)
    def _():
        C = 384
        def flush(slot, base):
            return pltpu.make_async_copy(stage.at[slot], gw_ref.at[pl.ds(base, C)], osem.at[slot])
        stage[0] = dot(e_s[:, 0:C], z_s[...], TN).astype(bf16); flush(0, 4 * D).start()
        stage[1] = dot(e_s[:, C:2 * C], z_s[...], TN).astype(bf16); flush(1, 4 * D + C).start()
        def grads(lhs, rhs, width, base):
            def step(r, _):
                slot = lax.rem(r, 2)
                at = pl.multiple_of(r * C, C)
                v = dot(lhs[:, pl.ds(at, C)], rhs[...], TN).astype(bf16)
                flush(slot, base).wait()
                stage[slot] = v
                flush(slot, pl.multiple_of(base + at, C)).start()
                return 0
            lax.fori_loop(0, width // C, step, 0)
        grads(cc_s, da_s, D, 3 * D)
        grads(du_s, n1_s, FF, 5 * D)
        grads(g_s, df_s, FF, 5 * D + FF)
        flush(0, 0).wait(); flush(1, 0).wait()

def ffn(plan, pieces, place, labels, exits, count, cls, x, ctx, og, vec, total):
    n = len(pieces); T = x.shape[0]; tiles = T // TILE; low = plan.tail_start
    tok = lambda dt: pl.BlockSpec((TILE, D), lambda i: (i, 0))
    return pl.pallas_call(
        functools.partial(ffn_kernel, plan, n, tiles, low), grid=(tiles,), name="ffn",
        in_specs=[SMEM] * 5 + [tok(0)] * 3 + [pl.BlockSpec((16, D), lambda i: (0, 0))] + [HBM] * n,
        out_specs=[tok(0), tok(0), tok(0), pl.BlockSpec((16, D), lambda i: (0, 0)), pl.BlockSpec((R, 128), lambda i: (0, 0)), ANY],
        out_shape=[jax.ShapeDtypeStruct((T, D), bf16), jax.ShapeDtypeStruct((T, D), f32), jax.ShapeDtypeStruct((T, D), bf16), jax.ShapeDtypeStruct((16, D), f32), jax.ShapeDtypeStruct((R, 128), f32), jax.ShapeDtypeStruct((total, D), bf16)],
        scratch_shapes=[pltpu.VMEM((MROWS - low, D), bf16), pltpu.SemaphoreType.DMA((len(plan.spans),)),
            pltpu.VMEM((T, FF), bf16), pltpu.VMEM((T, FF), bf16), pltpu.VMEM((T, D), bf16), pltpu.VMEM((T, D), bf16), pltpu.VMEM((T, D), bf16), pltpu.VMEM((T, D), bf16),
            pltpu.VMEM((TILE, FF), f32), pltpu.VMEM((TILE, D), f32), pltpu.VMEM((R * (T // L), D), bf16), pltpu.VMEM((R * (T // L), D), bf16),
            pltpu.VMEM((2, 384, D), bf16), pltpu.SemaphoreType.DMA((2,))],
        compiler_params=pltpu.CompilerParams(vmem_limit_bytes=60 << 20),
        cost_estimate=pl.CostEstimate(flops=33 * 10 ** 9, bytes_accessed=40 * 10 ** 6, transcendentals=6 * 10 ** 6),
    )(place, labels, exits, count, cls, x, ctx, og, vec, *pieces)

def attn_bwd_kernel(plan, n, S, place, lens, x_ref, qkv_ref, dc_ref, c_ref, st_ref, dh1_ref, *refs):
    pieces = refs[:n]; gw_in, dx_ref, vg_ref, gw_ref, w, sems, d_s, x_s, stage, osem = refs[n:]
    s = pl.program_id(0)
    ld = Loads(plan, pieces, place, w, sems, 0, plan.head_end)
    @pl.when(s == 0)
    def _():
        ld.start()
        vg_ref[...] = jnp.zeros_like(vg_ref)
    rows = pl.ds(pl.multiple_of(s * L, L), L)
    x_s[rows] = x_ref[0]
    length = lens[s]
    low = lax.broadcasted_iota(jnp.int32, (L, 128), 1) < HD
    valid = lax.broadcasted_iota(jnp.int32, (L, 1), 0) < length
    scale = LOG2E * HD ** -0.5
    for p in range(H // 2):
        sl = slice(p * 128, (p + 1) * 128)
        q2 = qkv_ref[0, :, sl]; k2 = qkv_ref[0, :, D + p * 128:D + (p + 1) * 128]; v2 = qkv_ref[0, :, 2 * D + p * 128:2 * D + (p + 1) * 128]
        dc2 = dc_ref[0, :, sl]
        prod = (dc2.astype(f32) * c_ref[0, :, sl].astype(f32)).T
        res = []
        for h in range(2):
            pick = low if h == 0 else ~low
            zero = jnp.zeros_like(q2)
            km = jnp.where(pick, k2, zero); vm = jnp.where(pick, v2, zero)
            delta = jnp.sum(prod[h * HD:(h + 1) * HD], axis=0, keepdims=True)
            st = jnp.where(valid, dot(km, q2, NT) * scale, MASK_FILL)
            pt = jnp.exp2(st - st_ref[0, 2 * p + h:2 * p + h + 1, :])
            dpt = dot(vm, dc2, NT)
            dst = (pt * (dpt - delta)).astype(bf16)
            res.append((dot(dst, k2, TN), dot(dst, q2), dot(pt.astype(bf16), dc2)))
        both = lambda t: jnp.where(low, res[0][t], res[1][t])
        d_s[rows, p * 128:(p + 1) * 128] = (both(0) * HD ** -0.5).astype(bf16)
        d_s[rows, D + p * 128:D + (p + 1) * 128] = (both(1) * HD ** -0.5).astype(bf16)
        d_s[rows, 2 * D + p * 128:2 * D + (p + 1) * 128] = both(2).astype(bf16)
    @pl.when(s == 0)
    def _(): ld.wait()
    dq, dk, dv = (d_s[rows, i * D:(i + 1) * D] for i in range(3))
    dx_ref[0] = (dh1_ref[0] + dot(dq, w[0:D], NT) + dot(dk, w[D:2 * D], NT) + dot(dv, w[2 * D:3 * D], NT)).astype(bf16)
    vg_ref[0:1] += jnp.sum(dq.astype(f32), axis=0, keepdims=True)
    vg_ref[1:2] += jnp.sum(dv.astype(f32), axis=0, keepdims=True)
    @pl.when(s == S - 1)
    def _():
        C = 384
        def flush(slot, base):
            return pltpu.make_async_copy(stage.at[slot], gw_ref.at[pl.ds(base, C)], osem.at[slot])
        for i in range(3):
            for r in range(2):
                v = dot(x_s[:, r * C:(r + 1) * C], d_s[:, i * D:(i + 1) * D], TN).astype(bf16)
                if i: flush(r, 0).wait()
                stage[r] = v
                flush(r, i * D + r * C).start()
        flush(0, 0).wait(); flush(1, 0).wait()

def attn_bwd(plan, pieces, place, lengths, tokens, qkv, dc, ctx, st, dh1, gw):
    n = len(pieces); S = tokens.shape[0]
    seq = lambda *sh: pl.BlockSpec((1,) + sh, lambda s: (s, 0, 0))
    return pl.pallas_call(
        functools.partial(attn_bwd_kernel, plan, n, S), grid=(S,), name="attn_bwd",
        in_specs=[SMEM, SMEM, seq(L, D), seq(L, 3 * D), seq(L, D), seq(L, D), seq(128, L), seq(L, D)] + [HBM] * n + [ANY],
        out_specs=[seq(L, D), pl.BlockSpec((8, D), lambda s: (0, 0)), ANY],
        out_shape=[jax.ShapeDtypeStruct((S, L, D), bf16), jax.ShapeDtypeStruct((8, D), f32), jax.ShapeDtypeStruct(gw.shape, bf16)],
        input_output_aliases={8 + n: 2},
        scratch_shapes=[pltpu.VMEM((plan.head_end, D), bf16), pltpu.SemaphoreType.DMA((len(plan.spans),)), pltpu.VMEM((S * L, 3 * D), bf16), pltpu.VMEM((S * L, D), bf16), pltpu.VMEM((2, 384, D), bf16), pltpu.SemaphoreType.DMA((2,))],
        compiler_params=pltpu.CompilerParams(vmem_limit_bytes=56 << 20),
        cost_estimate=pl.CostEstimate(flops=16 * 10 ** 9, bytes_accessed=24 * 10 ** 6, transcendentals=6 * 10 ** 6),
    )(place, lengths, tokens, qkv, dc, ctx, st, dh1, *pieces, gw)


FSDP = 16


def permute(axis, pairs, value, after):
    if after:
        value = lax.optimization_barrier((value, *after))[0]
    return lax.ppermute(value, axis, pairs)


def swap_core(value, *after):
    return permute("fsdp", [(i, i ^ 1) for i in range(FSDP)], value, after)


def swap_x(value, *after):
    return permute("fsdp", [(i, i ^ 2) for i in range(FSDP)], value, after)


def swap_y(value, *after):
    return permute("dp", [(0, 1), (1, 0)], value, after)


def next_z(value, *after):
    return permute("fsdp", [(i, (i + 4) % FSDP) for i in range(FSDP)], value, after)


def sum_small(value):
    value = value + swap_y(value)
    for bit in (1, 2, 4, 8):
        value = value + permute("fsdp", [(i, i ^ bit) for i in range(FSDP)], value, ())
    return value


def position():
    index = lax.axis_index("fsdp")
    return index // 4, index // 2 % 2, index % 2, lax.axis_index("dp")


def gather_pieces(shard, first):
    rows = shard.shape[0]
    plan = Plan([], rows, first)
    c, e, spans = first, plan.part_e, plan.spans
    size_e = rows - 2 * c
    rep = lax.axis_index("dp")
    low_e = shard[2 * c :]
    my_c = lax.dynamic_slice_in_dim(shard, rep * c, c)
    my_e = lax.dynamic_slice_in_dim(low_e, rep * (size_e - e), e)
    x0c, x0e = swap_x(my_c), swap_x(low_e)
    zc1, ze1 = next_z(my_c), next_z(my_e)
    ye1 = swap_y(ze1)
    xc1 = swap_x(zc1, x0c)
    zc2 = next_z(zc1, x0c)
    ze2 = next_z(ze1, x0e)
    y0 = swap_y(x0c)
    xe1 = swap_x(jnp.concatenate([ze1, ye1]), x0e)
    yc1 = swap_y(jnp.concatenate([zc1, xc1]))
    ye2 = swap_y(ze2, y0)
    xc2 = swap_x(zc2, xc1)
    zc3 = next_z(zc2, xc1)
    ze3 = next_z(ze2, xe1)
    xe2 = swap_x(jnp.concatenate([ze2, ye2]), xe1)
    ye3 = swap_y(ze3, yc1)
    yc2 = swap_y(jnp.concatenate([zc2, xc2]), yc1)
    xc3 = swap_x(zc3, xc2)
    xe3 = swap_x(jnp.concatenate([ze3, ye3]), xe2)
    yc3 = swap_y(jnp.concatenate([zc3, xc3]), yc2)
    pieces = []

    def both(value, *parts):
        for other_core, piece in ((0, value), (1, swap_core(value))):
            for start, count, steps, other_x, part in parts:
                spans.append((len(pieces), start, count, (steps, other_x, other_core, part)))
            pieces.append(piece)

    both(shard, (0, rows, 0, 0, "all"))
    both(x0c, (0, c, 0, 1, "c_mine"))
    both(x0e, (0, size_e, 0, 1, "e"))
    both(y0, (0, c, 0, 1, "c_other"))
    rounds = ((zc1, ze1, xc1, ye1, yc1, xe1), (zc2, ze2, xc2, ye2, yc2, xe2), (zc3, ze3, xc3, ye3, yc3, xe3))
    for k, (zc, ze, xc, ye, yc, xe) in enumerate(rounds, 1):
        both(zc, (0, c, k, 0, "c_mine"))
        both(ze, (0, e, k, 0, "e_mine"))
        both(xc, (0, c, k, 1, "c_mine"))
        both(ye, (0, size_e - e, k, 0, "e_other"))
        both(yc, (0, c, k, 0, "c_other"), (c, c, k, 1, "c_other"))
        both(xe, (0, e, k, 1, "e_mine"), (e, size_e - e, k, 1, "e_other"))
    return pieces, plan


def add_low(a, b):
    return (a.astype(f32) + b.astype(f32)).astype(bf16)


def scatter_sum(grads, rows, first):
    c, e = first, rows // 2 - first
    z, x, core, rep = position()
    stacked = grads.reshape(4, 2, 2, rows, D)
    cut = lax.dynamic_slice_in_dim
    ring_c = ring_e = None
    last = {"x": [], "y": [], "z": []}

    def link(name, swap, value):
        done = last[name]
        got = swap(value, *done[-2:-1])
        done.append(got)
        return got

    for k in (1, 2, 3, 0):
        target = lax.rem(z - k + 4, 4)

        def pick(at_x, at_core):
            return lax.dynamic_slice(stacked, (target, at_x, at_core, 0, 0), (1, 1, 1, rows, D)).reshape(rows, D)

        got = swap_core(jnp.concatenate([pick(x, 1 - core), pick(1 - x, 1 - core)]))
        own, other = add_low(got[:rows], pick(x, core)), add_low(got[rows:], pick(1 - x, core))
        yc = link("y", swap_y, jnp.concatenate([cut(own, (1 - rep) * c, c), cut(other, (1 - rep) * c, c)]))
        xe = link("x", swap_x, other[2 * c :])
        own_c, other_c = add_low(cut(own, rep * c, c), yc[:c]), add_low(cut(other, rep * c, c), yc[c:])
        own_e = add_low(own[2 * c :], xe)
        xc = link("x", swap_x, other_c)
        ye = link("y", swap_y, cut(own_e, (1 - rep) * e, e))
        sum_c = own_c.astype(f32) + xc.astype(f32)
        sum_e = cut(own_e, rep * e, e).astype(f32) + ye.astype(f32)
        if ring_c is not None:
            sum_c, sum_e = sum_c + ring_c.astype(f32), sum_e + ring_e.astype(f32)
        sum_c, sum_e = sum_c.astype(bf16), sum_e.astype(bf16)
        if k:
            ring_c, ring_e = link("z", next_z, sum_c), link("z", next_z, sum_e)
    back = swap_y(jnp.concatenate([sum_c, sum_e]))
    order = lambda a, b: [jnp.where(rep == 0, a, b), jnp.where(rep == 0, b, a)]
    return jnp.concatenate(order(sum_c, back[:c]) + order(sum_e, back[c:]))


def row_rates(row_index):
    base_rate = D ** (-0.5)
    return jnp.where(
        (row_index >= 3 * D) & (row_index < 4 * D),
        8.0 * base_rate,
        jnp.where(row_index >= 5 * D + FF, 1.5 * FF ** (-0.5), base_rate),
    )


def adam_update(master, first_mom, second_mom, grad_in, rate, decay):
    first_new = BETA_ONE * first_mom + (1.0 - BETA_ONE) * grad_in
    second_new = BETA_TWO * second_mom + (1.0 - BETA_TWO) * grad_in * grad_in
    fix_one = 1.0 - BETA_ONE**STEP
    fix_two = 1.0 - BETA_TWO**STEP
    direction = first_new / fix_one / (jnp.sqrt(second_new / fix_two) + ADAM_EPS)
    master_new = master - rate * (direction + decay * master)
    return (master_new, first_new, second_new)


def on_device(
    paths,
    tokens,
    out_grad,
    lengths,
    labels,
    exit_layers,
    mat_master,
    mat_first,
    mat_second,
    vec_master,
    vec_first,
    vec_second,
    cls_bias,
    cls_first,
    cls_second,
):
    seqs, toks = tokens.shape[0], tokens.shape[0] * L
    shard_rows, lanes = mat_master.shape[0], vec_master.shape[1]
    index = lax.axis_index("fsdp")
    place = jnp.stack(position()).astype(jnp.int32)
    active = jnp.sum((exit_layers >= LAYER).astype(f32))
    mat_low, vec_low = mat_master.astype(bf16), vec_master.astype(bf16)
    if paths:
        placed = lax.dynamic_update_slice(jnp.zeros((16, D), bf16), vec_low, (0, lanes * index))
        placed = jnp.where(lax.axis_index("dp") == 0, placed, jnp.zeros_like(placed))
        small = sum_small(jnp.concatenate([placed, jnp.full((8, D), active).astype(bf16)]))
        vectors, active_count = small[:16].astype(f32), small[16, 0].astype(f32)
        pieces, plan = gather_pieces(mat_low, paths[0])
    else:
        pieces = [lax.all_gather(mat_low, "fsdp", axis=0, tiled=True)]
        plan = Plan([(0, 0, MROWS, 0)], 3 * D)
        vectors = lax.all_gather(vec_low, "fsdp", axis=1, tiled=True).astype(f32)
        active_count = lax.psum(active, ("dp", "fsdp"))
    qkv, context, stats = attn_fwd(plan, pieces, place, lengths, tokens, vectors)
    block_out, grad_attn, grad_ctx, vec_grad, sums, mat_grad = ffn(
        plan,
        pieces,
        place,
        labels,
        exit_layers,
        active_count.reshape(1),
        cls_bias,
        tokens.reshape(toks, D),
        context.reshape(toks, D),
        out_grad.reshape(toks, D),
        vectors,
        MROWS,
    )
    input_grad, head_grad, mat_grad = attn_bwd(
        plan,
        pieces,
        place,
        lengths,
        tokens,
        qkv,
        grad_ctx.reshape(seqs, L, D),
        context,
        stats,
        grad_attn.reshape(seqs, L, D),
        mat_grad,
    )
    vec_grad = jnp.concatenate([head_grad[:2], vec_grad[2:]])
    sums = jnp.sum(sums, axis=0)
    if paths:
        mat_total = scatter_sum(mat_grad, shard_rows, paths[1]).astype(f32)
        small = sum_small(jnp.concatenate([vec_grad, jnp.pad(sums[None], ((0, 7), (0, D - 128)))]))
        vec_total = lax.dynamic_slice(small, (0, lanes * index), (16, lanes))
        sums = small[16, :4]
    else:
        part = lax.psum_scatter(mat_grad, "fsdp", scatter_dimension=0, tiled=True)
        mat_total = lax.psum(part, "dp").astype(f32)
        part = lax.psum_scatter(vec_grad.astype(bf16), "fsdp", scatter_dimension=1, tiled=True)
        vec_total = lax.psum(part, "dp").astype(f32)
        sums = lax.psum(sums[:4], ("dp", "fsdp"))
    ramp_loss = sums[0] / active_count
    cls_grad = sums[1:4] / active_count
    rates = row_rates(index * shard_rows + jnp.arange(shard_rows))[:, None]
    mat_new, mat_first_new, mat_second_new = adam_update(
        mat_master, mat_first, mat_second, mat_total, rates, WEIGHT_DECAY
    )
    vec_new, vec_first_new, vec_second_new = adam_update(
        vec_master, vec_first, vec_second, vec_total, VEC_RATE, 0.0
    )
    cls_new, cls_first_new, cls_second_new = adam_update(
        cls_bias, cls_first, cls_second, cls_grad, VEC_RATE, 0.0
    )
    return (
        block_out.reshape(seqs, L, D),
        input_grad,
        ramp_loss,
        mat_new,
        mat_first_new,
        mat_second_new,
        mat_new.astype(bf16),
        vec_new,
        vec_first_new,
        vec_second_new,
        vec_new.astype(bf16),
        cls_new,
        cls_first_new,
        cls_second_new,
    )


def solution(mesh):
    rows = P(("dp", "fsdp"), None, None)
    each = P(("dp", "fsdp"))
    mat, vec = P("fsdp", None), P(None, "fsdp")
    paths = (160, 160) if (mesh.shape["dp"], mesh.shape["fsdp"]) == (2, FSDP) else None
    return jax.shard_map(
        functools.partial(on_device, paths),
        mesh=mesh,
        in_specs=(rows, rows, each, each, each, mat, mat, mat, vec, vec, vec, P(), P(), P()),
        out_specs=(rows, rows, P(), mat, mat, mat, mat, vec, vec, vec, vec, P(), P(), P()),
        check_vma=False,
    )
```

```python
import functools
import math

import jax
import jax.numpy as jnp
from jax import lax
from jax.experimental import pallas as pl
from jax.experimental.pallas import tpu as pltpu
from jax.sharding import PartitionSpec as P

D, H, HD, FF, NCLS, L = 768, 12, 64, 3072, 3, 512
LAYER = 6
STEP = 10
BETA_ONE = 0.9
BETA_TWO = 0.999
ADAM_EPS = 1e-08
WEIGHT_DECAY = 0.01
VEC_RATE = 0.5
LN_EPS = 1e-12
MASK_FILL = -1e9
LOG2E = 1.4426950408889634
f32, bf16 = jnp.float32, jnp.bfloat16
NN = (((1,), (0,)), ((), ()))
NT = (((1,), (1,)), ((), ()))
TN = (((0,), (0,)), ((), ()))
def dot(a, b, dims=NN):
    return lax.dot_general(a, b, dims, preferred_element_type=f32)
ANY = pl.BlockSpec(memory_space=pl.ANY)
VMEM = pl.BlockSpec(memory_space=pltpu.VMEM)
HBM = pl.BlockSpec(memory_space=pltpu.HBM)
MROWS = 5 * D + 2 * FF
EARLY = 128
CHUNK = 384
SMEM = pl.BlockSpec(memory_space=pltpu.SMEM)
TILE = 256
R = 16
ERF_P = 0.3275911
ERF_A = (0.254829592, -0.284496736, 1.421413741, -1.453152027, 1.061405429)

class Loads:
    def __init__(self, plan, refs, place, dst, sems, low, high):
        self.items = []
        for j, (piece, src, count, row) in enumerate(plan.spans):
            if isinstance(row, int):
                first, last = max(row, low), min(row + count, high)
                if first >= last:
                    continue
                cond = None
                source = refs[piece].at[pl.ds(src + first - row, last - first)]
                target = dst.at[pl.ds(first - low, last - first)]
            else:
                shard, at = plan.locate(row, place)
                cond = (shard * plan.rows >= low) & (shard * plan.rows < high)
                source = refs[piece].at[pl.ds(src, count)]
                target = dst.at[pl.ds(pl.multiple_of(jnp.where(cond, at - low, 0), 16), count)]
            self.items.append((cond, pltpu.make_async_copy(source, target, sems.at[j])))

    def start(self):
        for cond, copy in self.items:
            if cond is None:
                copy.start()
            else:
                pl.when(cond)(copy.start)

    def wait(self):
        for cond, copy in self.items:
            if cond is None:
                copy.wait()
            else:
                pl.when(cond)(copy.wait)


class Plan:
    def __init__(self, spans, rows, parts=(0, 0, 0)):
        self.spans, self.rows, self.parts = spans, rows, parts
        self.head_end = -(-3 * D // rows) * rows
        self.tail_start = 3 * D // rows * rows

    def locate(self, where, place):
        steps, other_x, other_core, part = where
        z, x, core, rep = (place[i] for i in range(4))
        flip = lambda bit, other: 1 - bit if other else bit
        shard = (lax.rem(z - steps + 4, 4) * 2 + flip(x, other_x)) * 2 + flip(core, other_core)
        a, c, e = self.parts
        base = {
            "all": 0,
            "a": 0,
            "c_mine": a + rep * c,
            "c_other": a + (1 - rep) * c,
            "e": a + 2 * c,
            "e_late": a + 2 * c + EARLY,
            "e_mine": a + 2 * c + rep * e,
            "e_other": a + 2 * c + (1 - rep) * e,
        }[part]
        return shard, shard * self.rows + base


class Layout:
    def __init__(self, rows, half):
        self.rows, self.half = rows, half
        self.shapes = [jax.ShapeDtypeStruct((2 * rows, D), bf16)] * 8 if half else [jax.ShapeDtypeStruct((MROWS, D), bf16)]

    def write(self, place, staged, low, targets, sem, first, count):
        def start(target, at, rows, row):
            pltpu.make_async_copy(staged.at[pl.ds(at - low, rows)], target.at[pl.ds(row, rows)], sem).start()

        if not self.half:
            start(targets[0], first, count, first)
            return
        z, x, core, rep = (place[i] for i in range(4))
        rows, half = self.rows, self.half
        for shard in range(first // rows, -(-(first + count) // rows)):
            far_x, far_core = jnp.abs(x - shard // 2 % 2), jnp.abs(core - shard % 2)
            group = far_core * 4 + lax.rem(z - shard // 4 + 4, 4)
            runs = (
                (0, half, rep * 2 * half + far_x * half),
                (half, half, (1 - rep) * 2 * half + far_x * half),
                (2 * half, rows - 2 * half, 4 * half + (1 - far_x) * (rows - 2 * half)),
            )

            def put(target, shard=shard, runs=runs):
                for inner, size, row in runs:
                    begin = max(first, shard * rows + inner)
                    end = min(first + count, shard * rows + inner + size)
                    if begin < end:
                        start(target, begin, end - begin, pl.multiple_of(row + begin - shard * rows - inner, 16))

            for index, target in enumerate(targets):
                pl.when(group == index)(functools.partial(put, target))

    def wait(self, staged, low, targets, sem, first, count):
        rows = staged.at[pl.ds(first - low, count)]
        pltpu.make_async_copy(rows, rows, sem).wait()


def attn_fwd_kernel(plan, n, place, lens, x_ref, vec_ref, *refs):
    pieces = refs[:n]; qkv_ref, ctx_ref, st_ref, w, sems = refs[n:]
    s = pl.program_id(0)
    @pl.when(s == 0)
    def _():
        ld = Loads(plan, pieces, place, w, sems, 0, plan.head_end)
        ld.start(); ld.wait()
    x = x_ref[0]
    for i, b in ((0, 0), (1, None), (2, 1)):
        r = dot(x, w[i * D:(i + 1) * D])
        if b is not None: r = r + vec_ref[b:b + 1]
        qkv_ref[0, :, i * D:(i + 1) * D] = r.astype(bf16)
    length = lens[s]
    lane = lax.broadcasted_iota(jnp.int32, (L, 128), 1)
    low = lane < HD
    valid = lax.broadcasted_iota(jnp.int32, (1, L), 1) < length
    ones = jnp.ones((L, 128), bf16)
    stats = jnp.zeros((L, 128), f32)
    scale = LOG2E * HD ** -0.5
    for p in range(H // 2):
        q2 = qkv_ref[0, :, p * 128:(p + 1) * 128]
        k2 = qkv_ref[0, :, D + p * 128:D + (p + 1) * 128]
        v2 = qkv_ref[0, :, 2 * D + p * 128:2 * D + (p + 1) * 128]
        va = jnp.concatenate([v2, ones], axis=1)
        outs = []
        for h in range(2):
            qm = jnp.where(low if h == 0 else ~low, q2, jnp.zeros_like(q2))
            sc = jnp.where(valid, dot(qm, k2, NT) * scale, MASK_FILL)
            top = jnp.max(sc, axis=1, keepdims=True)
            e = jnp.exp2(sc - top).astype(bf16)
            o = dot(e, va)
            tot = o[:, 128:]
            outs.append(o[:, :128] / tot)
            stats = jnp.where(lane == 2 * p + h, top + jnp.log2(tot), stats)
        ctx_ref[0, :, p * 128:(p + 1) * 128] = jnp.where(low, outs[0], outs[1]).astype(bf16)
    st_ref[0] = stats.T

def attn_fwd(plan, pieces, place, lengths, tokens, vec):
    n = len(pieces); S = tokens.shape[0]
    return pl.pallas_call(
        functools.partial(attn_fwd_kernel, plan, n), grid=(S,), name="attn_fwd",
        in_specs=[SMEM, SMEM, pl.BlockSpec((1, L, D), lambda s: (s, 0, 0)), pl.BlockSpec((16, D), lambda s: (0, 0))] + [HBM] * n,
        out_specs=[pl.BlockSpec((1, L, 3 * D), lambda s: (s, 0, 0)), pl.BlockSpec((1, L, D), lambda s: (s, 0, 0)), pl.BlockSpec((1, 128, L), lambda s: (s, 0, 0))],
        out_shape=[jax.ShapeDtypeStruct((S, L, 3 * D), bf16), jax.ShapeDtypeStruct((S, L, D), bf16), jax.ShapeDtypeStruct((S, 128, L), f32)],
        scratch_shapes=[pltpu.VMEM((plan.head_end, D), bf16), pltpu.SemaphoreType.DMA((len(plan.spans),))],
        compiler_params=pltpu.CompilerParams(vmem_limit_bytes=50 << 20),
        cost_estimate=pl.CostEstimate(flops=8 * 10 ** 9, bytes_accessed=14 * 10 ** 6, transcendentals=6 * 10 ** 6),
    )(place, lengths, tokens, vec, *pieces)

def norm(h):
    mu = jnp.mean(h, axis=1, keepdims=True)
    c = h - mu
    r = lax.rsqrt(jnp.mean(c * c, axis=1, keepdims=True) + LN_EPS)
    return c * r, r

def norm_back(g, xh, r, gain):
    a = g * gain
    return r * (a - jnp.mean(a, axis=1, keepdims=True) - xh * jnp.mean(a * xh, axis=1, keepdims=True))

def gelu_both(u):
    t = 1.0 / (1.0 + (ERF_P * 2 ** -0.5) * jnp.abs(u))
    bell = jnp.exp2(u * u * (-0.5 * LOG2E))
    a = [0.5 * v for v in ERF_A]
    poly = t * (a[0] + t * (a[1] + t * (a[2] + t * (a[3] + t * a[4]))))
    tail = poly * bell
    phi = jnp.where(u < 0, tail, 1.0 - tail)
    g = u * phi
    return g, phi + (u * bell) * (2 * math.pi) ** -0.5

def ffn_kernel(plan, layout, n, tiles, low, place, labels, exits, count, cls, x_ref, c_ref, og_ref, vec_ref, *refs):
    m = n + 5 + len(layout.shapes)
    pieces, gw_refs = refs[:n], refs[n + 5:m]
    out_ref, dh1_ref, dc_ref, vg_ref, sc_ref = refs[n:n + 5]
    w, sems, g_s, du_s, n1_s, df_s, da_s, cc_s, gp_s, dy_s, e_s, z_s, osem = refs[m:]
    i = pl.program_id(0)
    ld = Loads(plan, pieces, place, w, sems, low, MROWS)
    @pl.when(i == 0)
    def _():
        ld.start()
        vg_ref[...] = jnp.zeros_like(vg_ref); sc_ref[...] = jnp.zeros_like(sc_ref)
        ld.wait()
    wo, wp, w1, w2 = 3 * D - low, 4 * D - low, 5 * D - low, 5 * D + FF - low
    vrow = lambda r: vec_ref[r:r + 1]
    rows = pl.ds(pl.multiple_of(i * TILE, TILE), TILE)
    c = c_ref[...]
    cc_s[rows] = c
    h1 = x_ref[...].astype(f32) + (dot(c, w[wo:wo + D]) + vrow(2))
    xh1, r1 = norm(h1)
    n1 = xh1 * vrow(3) + vrow(4)
    n1b = n1.astype(bf16)
    n1_s[rows] = n1b
    f = None
    for j in range(FF // D):
        u = dot(n1b, w[w1 + j * D:w1 + (j + 1) * D], NT) + vrow(9 + j)
        g, gp = gelu_both(u)
        gb = g.astype(bf16)
        g_s[rows, j * D:(j + 1) * D] = gb
        gp_s[:, j * D:(j + 1) * D] = gp
        part = dot(gb, w[w2 + j * D:w2 + (j + 1) * D])
        f = part if f is None else f + part
    xh2, r2 = norm(n1 + (f + vrow(5)))
    yb = (xh2 * vrow(6) + vrow(7)).astype(bf16)
    out_ref[...] = yb
    dy_s[...] = og_ref[...].astype(f32)
    per = L // TILE
    @pl.when(lax.rem(i, per) == 0)
    def _():
        s = i // per
        head = lax.broadcasted_iota(jnp.int32, (R, 1), 0) == 0
        act = jnp.where(head, jnp.where(exits[s] >= LAYER, 1.0, 0.0), 0.0)
        e8 = jnp.where(head, yb[:R].astype(f32), 0.0).astype(bf16)
        pool = jnp.tanh(dot(e8, w[wp:wp + D]) + vrow(8))
        pb = pool.astype(bf16).astype(f32)
        lg = [jnp.sum(pb * vrow(13 + k), axis=1, keepdims=True) + cls[k] for k in range(NCLS)]
        top = jnp.maximum(jnp.maximum(lg[0], lg[1]), lg[2])
        lse = top + jnp.log(jnp.exp(lg[0] - top) + jnp.exp(lg[1] - top) + jnp.exp(lg[2] - top))
        hot = [jnp.where(labels[s] == k, 1.0, 0.0) for k in range(NCLS)]
        ce = act * (lse - (lg[0] * hot[0] + lg[1] * hot[1] + lg[2] * hot[2]))
        err = [act * (jnp.exp(lg[k] - lse) - hot[k]) for k in range(NCLS)]
        lane = lax.broadcasted_iota(jnp.int32, (R, 128), 1)
        got = jnp.where(lane == 0, ce, 0.0)
        for k in range(NCLS): got = jnp.where(lane == 1 + k, err[k], got)
        sc_ref[...] += got
        dl = [(err[k] / count[0]).astype(bf16).astype(f32) for k in range(NCLS)]
        gpool = dl[0] * vrow(13) + dl[1] * vrow(14) + dl[2] * vrow(15)
        dz = (gpool * (1.0 - pool * pool)).astype(bf16)
        srow = pl.ds(pl.multiple_of(s * R, R), R)
        e_s[srow] = e8; z_s[srow] = dz
        vg_ref[8:9] += jnp.sum(dz.astype(f32), axis=0, keepdims=True)
        for k in range(NCLS): vg_ref[13 + k:14 + k] += jnp.sum(dl[k] * pb, axis=0, keepdims=True)
        dy_s[0:R] += dot(dz, w[wp:wp + D], NT)
    dy = dy_s[...]
    def vsum(r, v): vg_ref[r:r + 1] += jnp.sum(v, axis=0, keepdims=True)
    vsum(6, dy * xh2); vsum(7, dy)
    dh2 = norm_back(dy, xh2, r2, vrow(6))
    dfb = dh2.astype(bf16)
    df_s[rows] = dfb
    vsum(5, dfb.astype(f32))
    dn1 = dh2
    for j in range(FF // D):
        du = (dot(dfb, w[w2 + j * D:w2 + (j + 1) * D], NT) * gp_s[:, j * D:(j + 1) * D]).astype(bf16)
        du_s[rows, j * D:(j + 1) * D] = du
        vsum(9 + j, du.astype(f32))
        dn1 = dn1 + dot(du, w[w1 + j * D:w1 + (j + 1) * D])
    vsum(3, dn1 * xh1); vsum(4, dn1)
    dh1 = norm_back(dn1, xh1, r1, vrow(3))
    dh1_ref[...] = dh1
    dab = dh1.astype(bf16)
    da_s[rows] = dab
    vsum(2, dab.astype(f32))
    dc_ref[...] = dot(dab, w[wo:wo + D], NT).astype(bf16)
    @pl.when(i == tiles - 1)
    def _():
        for lhs, rhs, width, base in ((e_s, z_s, D, 4 * D), (cc_s, da_s, D, 3 * D), (du_s, n1_s, FF, 5 * D), (g_s, df_s, FF, 5 * D + FF)):

            def step(r, carry, lhs=lhs, rhs=rhs, base=base):
                at = pl.multiple_of(r * CHUNK, CHUNK)
                w[pl.ds(pl.multiple_of(base - low + at, 16), CHUNK)] = dot(lhs[:, pl.ds(at, CHUNK)], rhs[...], TN).astype(bf16)
                return carry

            lax.fori_loop(0, width // CHUNK, step, 0)
            layout.write(place, w, low, gw_refs, osem.at[0], base, width)
        layout.wait(w, low, gw_refs, osem.at[0], 3 * D, MROWS - 3 * D)

def ffn(plan, layout, pieces, place, labels, exits, count, cls, x, ctx, og, vec):
    n = len(pieces); T = x.shape[0]; tiles = T // TILE; low = plan.tail_start
    tok = lambda dt: pl.BlockSpec((TILE, D), lambda i: (i, 0))
    return pl.pallas_call(
        functools.partial(ffn_kernel, plan, layout, n, tiles, low), grid=(tiles,), name="ffn",
        in_specs=[SMEM] * 5 + [tok(0)] * 3 + [pl.BlockSpec((16, D), lambda i: (0, 0))] + [HBM] * n,
        out_specs=[tok(0), tok(0), tok(0), pl.BlockSpec((16, D), lambda i: (0, 0)), pl.BlockSpec((R, 128), lambda i: (0, 0))] + [ANY] * len(layout.shapes),
        out_shape=[jax.ShapeDtypeStruct((T, D), bf16), jax.ShapeDtypeStruct((T, D), f32), jax.ShapeDtypeStruct((T, D), bf16), jax.ShapeDtypeStruct((16, D), f32), jax.ShapeDtypeStruct((R, 128), f32)] + layout.shapes,
        scratch_shapes=[pltpu.VMEM((MROWS - low, D), bf16), pltpu.SemaphoreType.DMA((len(plan.spans),)),
            pltpu.VMEM((T, FF), bf16), pltpu.VMEM((T, FF), bf16), pltpu.VMEM((T, D), bf16), pltpu.VMEM((T, D), bf16), pltpu.VMEM((T, D), bf16), pltpu.VMEM((T, D), bf16),
            pltpu.VMEM((TILE, FF), f32), pltpu.VMEM((TILE, D), f32), pltpu.VMEM((R * (T // L), D), bf16), pltpu.VMEM((R * (T // L), D), bf16),
            pltpu.SemaphoreType.DMA((1,))],
        compiler_params=pltpu.CompilerParams(vmem_limit_bytes=60 << 20),
        cost_estimate=pl.CostEstimate(flops=33 * 10 ** 9, bytes_accessed=40 * 10 ** 6, transcendentals=6 * 10 ** 6),
    )(place, labels, exits, count, cls, x, ctx, og, vec, *pieces)

def attn_bwd_kernel(plan, layout, n, S, place, lens, x_ref, qkv_ref, dc_ref, c_ref, st_ref, dh1_ref, *refs):
    m = len(layout.shapes)
    pieces = refs[:n]
    dx_ref, vg_ref = refs[n + m:n + m + 2]
    gw_refs = refs[n + m + 2:n + 2 * m + 2]
    w, sems, d_s, x_s, osem = refs[n + 2 * m + 2:]
    s = pl.program_id(0)
    ld = Loads(plan, pieces, place, w, sems, 0, plan.head_end)
    @pl.when(s == 0)
    def _():
        ld.start()
        vg_ref[...] = jnp.zeros_like(vg_ref)
    rows = pl.ds(pl.multiple_of(s * L, L), L)
    x_s[rows] = x_ref[0]
    length = lens[s]
    low = lax.broadcasted_iota(jnp.int32, (L, 128), 1) < HD
    valid = lax.broadcasted_iota(jnp.int32, (L, 1), 0) < length
    scale = LOG2E * HD ** -0.5
    for p in range(H // 2):
        sl = slice(p * 128, (p + 1) * 128)
        q2 = qkv_ref[0, :, sl]; k2 = qkv_ref[0, :, D + p * 128:D + (p + 1) * 128]; v2 = qkv_ref[0, :, 2 * D + p * 128:2 * D + (p + 1) * 128]
        dc2 = dc_ref[0, :, sl]
        prod = (dc2.astype(f32) * c_ref[0, :, sl].astype(f32)).T
        res = []
        for h in range(2):
            pick = low if h == 0 else ~low
            zero = jnp.zeros_like(q2)
            km = jnp.where(pick, k2, zero); vm = jnp.where(pick, v2, zero)
            delta = jnp.sum(prod[h * HD:(h + 1) * HD], axis=0, keepdims=True)
            st = jnp.where(valid, dot(km, q2, NT) * scale, MASK_FILL)
            pt = jnp.exp2(st - st_ref[0, 2 * p + h:2 * p + h + 1, :])
            dpt = dot(vm, dc2, NT)
            dst = (pt * (dpt - delta)).astype(bf16)
            res.append((dot(dst, k2, TN), dot(dst, q2), dot(pt.astype(bf16), dc2)))
        both = lambda t: jnp.where(low, res[0][t], res[1][t])
        d_s[rows, p * 128:(p + 1) * 128] = (both(0) * HD ** -0.5).astype(bf16)
        d_s[rows, D + p * 128:D + (p + 1) * 128] = (both(1) * HD ** -0.5).astype(bf16)
        d_s[rows, 2 * D + p * 128:2 * D + (p + 1) * 128] = both(2).astype(bf16)
    @pl.when(s == 0)
    def _(): ld.wait()
    dq, dk, dv = (d_s[rows, i * D:(i + 1) * D] for i in range(3))
    dx_ref[0] = (dh1_ref[0] + dot(dq, w[0:D], NT) + dot(dk, w[D:2 * D], NT) + dot(dv, w[2 * D:3 * D], NT)).astype(bf16)
    vg_ref[0:1] += jnp.sum(dq.astype(f32), axis=0, keepdims=True)
    vg_ref[1:2] += jnp.sum(dv.astype(f32), axis=0, keepdims=True)
    @pl.when(s == S - 1)
    def _():
        for i in range(3):
            for at in range(0, D, CHUNK):
                w[i * D + at:i * D + at + CHUNK] = dot(x_s[:, at:at + CHUNK], d_s[:, i * D:(i + 1) * D], TN).astype(bf16)
            layout.write(place, w, 0, gw_refs, osem.at[0], i * D, D)
        layout.wait(w, 0, gw_refs, osem.at[0], 0, 3 * D)

def attn_bwd(plan, layout, pieces, place, lengths, tokens, qkv, dc, ctx, st, dh1, gw):
    n, m, S = len(pieces), len(gw), tokens.shape[0]
    seq = lambda *sh: pl.BlockSpec((1,) + sh, lambda s: (s, 0, 0))
    return pl.pallas_call(
        functools.partial(attn_bwd_kernel, plan, layout, n, S), grid=(S,), name="attn_bwd",
        in_specs=[SMEM, SMEM, seq(L, D), seq(L, 3 * D), seq(L, D), seq(L, D), seq(128, L), seq(L, D)] + [HBM] * n + [ANY] * m,
        out_specs=[seq(L, D), pl.BlockSpec((8, D), lambda s: (0, 0))] + [ANY] * m,
        out_shape=[jax.ShapeDtypeStruct((S, L, D), bf16), jax.ShapeDtypeStruct((8, D), f32)] + layout.shapes,
        input_output_aliases={8 + n + i: 2 + i for i in range(m)},
        scratch_shapes=[pltpu.VMEM((plan.head_end, D), bf16), pltpu.SemaphoreType.DMA((len(plan.spans),)), pltpu.VMEM((S * L, 3 * D), bf16), pltpu.VMEM((S * L, D), bf16), pltpu.SemaphoreType.DMA((1,))],
        compiler_params=pltpu.CompilerParams(vmem_limit_bytes=56 << 20),
        cost_estimate=pl.CostEstimate(flops=16 * 10 ** 9, bytes_accessed=24 * 10 ** 6, transcendentals=6 * 10 ** 6),
    )(place, lengths, tokens, qkv, dc, ctx, st, dh1, *pieces, *gw)


FSDP = 16


WAYS = {
    "x": ("fsdp", tuple((i, i ^ 2) for i in range(FSDP))),
    "y": ("dp", ((0, 1), (1, 0))),
    "z": ("fsdp", tuple((i, (i + 4) % FSDP) for i in range(FSDP))),
    "core": ("fsdp", tuple((i, i ^ 1) for i in range(FSDP))),
}
PARTS = (80, 128, 144)
HALF = 160


def hold(value, *others):
    return lax.optimization_barrier((value, *others))[0] if others else value


def send(way, *values):
    return lax.ppermute(values[0] if len(values) == 1 else jnp.concatenate(values), *WAYS[way])


def position():
    index = lax.axis_index("fsdp")
    return index // 4, index // 2 % 2, index % 2, lax.axis_index("dp")


def gather(shard, small):
    a, c, e = PARTS
    rows, rep = shard.shape[0], lax.axis_index("dp")
    cut = lax.dynamic_slice_in_dim
    all_a, all_e = shard[:a], shard[a + 2 * c :]
    my_c, my_e = cut(shard, a + rep * c, c), cut(shard, a + 2 * c + rep * e, e)
    late = 2 * e - EARLY
    zc, ze = (lambda k: z[k][:c]), (lambda k: z[k][c : c + e])
    z, za = {}, {}
    z[1] = send("z", my_c, my_e, small)
    x1 = send("x", all_a, my_c, all_e[:EARLY])
    z[2] = send("z", z[1])
    x2 = send("x", all_e[EARLY:], zc(1))
    y2 = send("y", x1[a : a + c], ze(1))
    za[1] = send("z", all_a, x1[:a])
    x3 = send("x", zc(2), ze(1), y2[c:])
    y3 = send("y", zc(1), x2[late:], ze(2))
    z[3] = send("z", hold(z[2], x2))
    za[2] = send("z", hold(za[1], y2, x2))
    small = small + z[1][c + e :] + z[2][c + e :] + z[3][c + e :]
    x4 = send("x", zc(3), ze(2), y3[2 * c :], small)
    y4 = send("y", zc(2), x3[:c], ze(3))
    za[3] = send("z", hold(za[2], y3, x3))
    small = small + x4[c + 2 * e :]
    x5 = send("x", ze(3), y4[2 * c :])
    y5 = send("y", zc(3), x4[:c], small)
    small = small + y5[2 * c :]
    za = {1: hold(za[1], x3, y3), 2: hold(za[2], x4, y4), 3: hold(za[3], x5, y5)}
    small = small + send("core", small)
    held = [(shard, ((0, rows, 0, 0, "all"),))]
    for k in (1, 2, 3):
        held.append((z[k], ((0, c, k, 0, "c_mine"), (c, e, k, 0, "e_mine"))))
        held.append((za[k], ((0, a, k, 0, "a"), (a, a, k, 1, "a"))))
    held.append((x1, ((0, a, 0, 1, "a"), (a, c, 0, 1, "c_mine"), (a + c, EARLY, 0, 1, "e"))))
    held.append((x2, ((0, late, 0, 1, "e_late"), (late, c, 1, 1, "c_mine"))))
    held.append((y2, ((0, c, 0, 1, "c_other"), (c, e, 1, 0, "e_other"))))
    for k, x_got, y_got in ((2, x3, y3), (3, x4, y4)):
        held.append((x_got, ((0, c, k, 1, "c_mine"), (c, e, k - 1, 1, "e_mine"), (c + e, e, k - 1, 1, "e_other"))))
        held.append((y_got, ((0, c, k - 1, 0, "c_other"), (c, c, k - 1, 1, "c_other"), (2 * c, e, k, 0, "e_other"))))
    held.append((x5, ((0, e, 3, 1, "e_mine"), (e, e, 3, 1, "e_other"))))
    held.append((y5, ((0, c, 3, 0, "c_other"), (c, c, 3, 1, "c_other"))))
    pieces, plan = [], Plan([], rows, PARTS)
    for value, parts in held:
        for other_core, piece in ((0, value), (1, send("core", value))):
            for start, count, steps, other_x, part in parts:
                plan.spans.append((len(pieces), start, count, (steps, other_x, other_core, part)))
            pieces.append(piece)
    return pieces, plan, small


def add_low(a, b):
    return (a.astype(f32) + b.astype(f32)).astype(bf16)


def scatter_sum(grads, small, sums, half):
    rows = grads[0].shape[0] // 2
    c, e = half, rows // 2 - half
    rep = lax.axis_index("dp")
    cut = lax.dynamic_slice_in_dim
    links = {"x": [], "y": [], "z": []}

    def link(name, *values):
        done = links[name]
        first = hold(values[0], *done[-2:-1])
        done.append(send(name, first, *values[1:]))
        return done[-1]

    def packed():
        high = sums.astype(bf16)
        low = (sums - high.astype(f32)).astype(bf16)
        return jnp.concatenate([small, jnp.stack([high, low] + [jnp.zeros_like(high)] * 6)])

    def added(others):
        total, total_sums = small.astype(f32), sums
        for other in others:
            total = total + other[:16].astype(f32)
            total_sums = total_sums + (other[16].astype(f32) + other[17].astype(f32))
        return total.astype(bf16), total_sums

    small, sums = added([send("core", packed())])
    rider, riders = packed(), []
    ring_c = ring_e = to_y = None
    for k in (1, 2, 3, 0):
        keep, got = grads[k], send("core", grads[4 + k])
        part = lambda first, count: add_low(keep[first : first + count], got[first : first + count])
        to_y = part(2 * c, 2 * c)
        yc = link("y", to_y)
        xe = link("x", part(4 * c, 2 * e))
        both_c = add_low(part(0, 2 * c), yc)
        own_e = add_low(part(4 * c + 2 * e, 2 * e), xe)
        if k == 0:
            small, sums = added(riders)
            xc = link("x", both_c[c:], packed())
            small, sums = added([xc[c:]])
        else:
            xc = link("x", both_c[c:])
        ye = link("y", cut(own_e, (1 - rep) * e, e))
        sum_c = both_c[:c].astype(f32) + xc[:c].astype(f32)
        sum_e = cut(own_e, rep * e, e).astype(f32) + ye.astype(f32)
        if ring_c is not None:
            sum_c, sum_e = sum_c + ring_c.astype(f32), sum_e + ring_e[:e].astype(f32)
        sum_c, sum_e = sum_c.astype(bf16), sum_e.astype(bf16)
        if k:
            ring_c, ring_e = link("z", sum_c), link("z", sum_e, rider)
            rider = ring_e[e:]
            riders.append(rider)
    back = send("y", sum_c, sum_e, packed())
    small, sums = added([back[c + e :]])
    order = lambda a, b: [jnp.where(rep == 0, a, b), jnp.where(rep == 0, b, a)]
    return jnp.concatenate(order(sum_c, back[:c]) + order(sum_e, back[c : c + e])), small, sums


def row_rates(row_index):
    base_rate = D ** (-0.5)
    return jnp.where(
        (row_index >= 3 * D) & (row_index < 4 * D),
        8.0 * base_rate,
        jnp.where(row_index >= 5 * D + FF, 1.5 * FF ** (-0.5), base_rate),
    )


def adam_update(master, first_mom, second_mom, grad_in, rate, decay):
    first_new = BETA_ONE * first_mom + (1.0 - BETA_ONE) * grad_in
    second_new = BETA_TWO * second_mom + (1.0 - BETA_TWO) * grad_in * grad_in
    fix_one = 1.0 - BETA_ONE**STEP
    fix_two = 1.0 - BETA_TWO**STEP
    direction = first_new / fix_one / (jnp.sqrt(second_new / fix_two) + ADAM_EPS)
    master_new = master - rate * (direction + decay * master)
    return (master_new, first_new, second_new)


def on_device(
    paths,
    tokens,
    out_grad,
    lengths,
    labels,
    exit_layers,
    mat_master,
    mat_first,
    mat_second,
    vec_master,
    vec_first,
    vec_second,
    cls_bias,
    cls_first,
    cls_second,
):
    seqs, toks = tokens.shape[0], tokens.shape[0] * L
    shard_rows, lanes = mat_master.shape[0], vec_master.shape[1]
    index = lax.axis_index("fsdp")
    place = jnp.stack(position()).astype(jnp.int32)
    active = jnp.sum((exit_layers >= LAYER).astype(f32))
    mat_low, vec_low = mat_master.astype(bf16), vec_master.astype(bf16)
    if paths:
        placed = lax.dynamic_update_slice(jnp.zeros((16, D), bf16), vec_low, (0, lanes * index))
        placed = jnp.where(lax.axis_index("dp") == 0, placed, jnp.zeros_like(placed))
        layout = Layout(shard_rows, HALF)
        pieces, plan, small = gather(mat_low, jnp.concatenate([placed, jnp.full((8, D), active).astype(bf16)]))
        vectors, active_count = small[:16].astype(f32), small[16, 0].astype(f32)
    else:
        pieces = [lax.all_gather(mat_low, "fsdp", axis=0, tiled=True)]
        plan, layout = Plan([(0, 0, MROWS, 0)], 3 * D), Layout(shard_rows, 0)
        vectors = lax.all_gather(vec_low, "fsdp", axis=1, tiled=True).astype(f32)
        active_count = lax.psum(active, ("dp", "fsdp"))
    qkv, context, stats = attn_fwd(plan, pieces, place, lengths, tokens, vectors)
    block_out, grad_attn, grad_ctx, vec_grad, sums, *mat_grad = ffn(
        plan,
        layout,
        pieces,
        place,
        labels,
        exit_layers,
        active_count.reshape(1),
        cls_bias,
        tokens.reshape(toks, D),
        context.reshape(toks, D),
        out_grad.reshape(toks, D),
        vectors,
    )
    input_grad, head_grad, *mat_grad = attn_bwd(
        plan,
        layout,
        pieces,
        place,
        lengths,
        tokens,
        qkv,
        grad_ctx.reshape(seqs, L, D),
        context,
        stats,
        grad_attn.reshape(seqs, L, D),
        mat_grad,
    )
    vec_grad = jnp.concatenate([head_grad[:2], vec_grad[2:]])
    sums = jnp.sum(sums, axis=0)
    if paths:
        mat_total, vec_total, sums = scatter_sum(mat_grad, vec_grad.astype(bf16), jnp.pad(sums, (0, D - 128)), HALF)
        mat_total = mat_total.astype(f32)
        vec_total = lax.dynamic_slice(vec_total, (0, lanes * index), (16, lanes)).astype(f32)
    else:
        part = lax.psum_scatter(mat_grad[0], "fsdp", scatter_dimension=0, tiled=True)
        mat_total = lax.psum(part, "dp").astype(f32)
        part = lax.psum_scatter(vec_grad.astype(bf16), "fsdp", scatter_dimension=1, tiled=True)
        vec_total = lax.psum(part, "dp").astype(f32)
        sums = lax.psum(sums[:4], ("dp", "fsdp"))
    ramp_loss = sums[0] / active_count
    cls_grad = sums[1:4] / active_count
    rates = row_rates(index * shard_rows + jnp.arange(shard_rows))[:, None]
    mat_new, mat_first_new, mat_second_new = adam_update(
        mat_master, mat_first, mat_second, mat_total, rates, WEIGHT_DECAY
    )
    vec_new, vec_first_new, vec_second_new = adam_update(
        vec_master, vec_first, vec_second, vec_total, VEC_RATE, 0.0
    )
    cls_new, cls_first_new, cls_second_new = adam_update(
        cls_bias, cls_first, cls_second, cls_grad, VEC_RATE, 0.0
    )
    return (
        block_out.reshape(seqs, L, D),
        input_grad,
        ramp_loss,
        mat_new,
        mat_first_new,
        mat_second_new,
        mat_new.astype(bf16),
        vec_new,
        vec_first_new,
        vec_second_new,
        vec_new.astype(bf16),
        cls_new,
        cls_first_new,
        cls_second_new,
    )


def solution(mesh):
    rows = P(("dp", "fsdp"), None, None)
    each = P(("dp", "fsdp"))
    mat, vec = P("fsdp", None), P(None, "fsdp")
    paths = (mesh.shape["dp"], mesh.shape["fsdp"]) == (2, FSDP)
    return jax.shard_map(
        functools.partial(on_device, paths),
        mesh=mesh,
        in_specs=(rows, rows, each, each, each, mat, mat, mat, vec, vec, vec, P(), P(), P()),
        out_specs=(rows, rows, P(), mat, mat, mat, mat, vec, vec, vec, vec, P(), P(), P()),
        check_vma=False,
    )
```

```python
import functools
import math

import jax
import jax.numpy as jnp
from jax import lax
from jax.experimental import pallas as pl
from jax.experimental.pallas import tpu as pltpu
from jax.sharding import PartitionSpec as P

D, H, HD, FF, NCLS, L = 768, 12, 64, 3072, 3, 512
LAYER = 6
STEP = 10
BETA_ONE = 0.9
BETA_TWO = 0.999
ADAM_EPS = 1e-08
WEIGHT_DECAY = 0.01
VEC_RATE = 0.5
LN_EPS = 1e-12
MASK_FILL = -1e9
LOG2E = 1.4426950408889634
f32, bf16 = jnp.float32, jnp.bfloat16
NN = (((1,), (0,)), ((), ()))
NT = (((1,), (1,)), ((), ()))
TN = (((0,), (0,)), ((), ()))
def dot(a, b, dims=NN):
    return lax.dot_general(a, b, dims, preferred_element_type=f32)
ANY = pl.BlockSpec(memory_space=pl.ANY)
VMEM = pl.BlockSpec(memory_space=pltpu.VMEM)
HBM = pl.BlockSpec(memory_space=pltpu.HBM)
MROWS = 5 * D + 2 * FF
EARLY = 128
CHUNK = 1536
UNITS = 1536
SMEM = pl.BlockSpec(memory_space=pltpu.SMEM)
TILE = 256
R = 16


class Loads:
    def __init__(self, plan, refs, place, dst, sems, low, high):
        self.items = []
        for j, (piece, src, count, row) in enumerate(plan.spans):
            if isinstance(row, int):
                first, last = max(row, low), min(row + count, high)
                if first >= last:
                    continue
                cond = None
                source = refs[piece].at[pl.ds(src + first - row, last - first)]
                target = dst.at[pl.ds(first - low, last - first)]
            else:
                shard, at = plan.locate(row, place)
                cond = (shard * plan.rows >= low) & (shard * plan.rows < high)
                source = refs[piece].at[pl.ds(src, count)]
                target = dst.at[pl.ds(pl.multiple_of(jnp.where(cond, at - low, 0), 16), count)]
            self.items.append((cond, pltpu.make_async_copy(source, target, sems.at[j])))

    def start(self):
        for cond, copy in self.items:
            if cond is None:
                copy.start()
            else:
                pl.when(cond)(copy.start)

    def wait(self):
        for cond, copy in self.items:
            if cond is None:
                copy.wait()
            else:
                pl.when(cond)(copy.wait)


class Plan:
    def __init__(self, spans, rows, parts=(0, 0, 0)):
        self.spans, self.rows, self.parts = spans, rows, parts
        self.head_end = -(-3 * D // rows) * rows
        self.tail_start = 3 * D // rows * rows

    def locate(self, where, place):
        steps, other_x, other_core, part = where
        z, x, core, rep = (place[i] for i in range(4))
        flip = lambda bit, other: 1 - bit if other else bit
        shard = (lax.rem(z - steps + 4, 4) * 2 + flip(x, other_x)) * 2 + flip(core, other_core)
        a, c, e = self.parts
        base = {
            "all": 0,
            "a": 0,
            "c_mine": a + rep * c,
            "c_other": a + (1 - rep) * c,
            "e": a + 2 * c,
            "e_late": a + 2 * c + EARLY,
            "e_mine": a + 2 * c + rep * e,
            "e_other": a + 2 * c + (1 - rep) * e,
        }[part]
        return shard, shard * self.rows + base


class Layout:
    def __init__(self, rows, half):
        self.rows, self.half = rows, half
        self.shapes = [jax.ShapeDtypeStruct((2 * rows, D), bf16)] * 8 if half else [jax.ShapeDtypeStruct((MROWS, D), bf16)]

    def write(self, place, staged, low, targets, sem, first, count):
        def start(target, at, rows, row):
            pltpu.make_async_copy(staged.at[pl.ds(at - low, rows)], target.at[pl.ds(row, rows)], sem).start()

        if not self.half:
            start(targets[0], first, count, first)
            return
        z, x, core, rep = (place[i] for i in range(4))
        rows, half = self.rows, self.half
        for shard in range(first // rows, -(-(first + count) // rows)):
            far_x, far_core = jnp.abs(x - shard // 2 % 2), jnp.abs(core - shard % 2)
            group = far_core * 4 + lax.rem(z - shard // 4 + 4, 4)
            runs = (
                (0, half, rep * 2 * half + far_x * half),
                (half, half, (1 - rep) * 2 * half + far_x * half),
                (2 * half, rows - 2 * half, 4 * half + (1 - far_x) * (rows - 2 * half)),
            )

            def put(target, shard=shard, runs=runs):
                for inner, size, row in runs:
                    begin = max(first, shard * rows + inner)
                    end = min(first + count, shard * rows + inner + size)
                    if begin < end:
                        start(target, begin, end - begin, pl.multiple_of(row + begin - shard * rows - inner, 16))

            for index, target in enumerate(targets):
                pl.when(group == index)(functools.partial(put, target))

    def wait(self, staged, low, targets, sem, first, count):
        rows = staged.at[pl.ds(first - low, count)]
        pltpu.make_async_copy(rows, rows, sem).wait()


def attn_fwd_kernel(plan, n, place, lens, x_ref, vec_ref, *refs):
    pieces = refs[:n]; qkv_ref, ctx_ref, st_ref, w, sems = refs[n:]
    s = pl.program_id(0)
    @pl.when(s == 0)
    def _():
        ld = Loads(plan, pieces, place, w, sems, 0, plan.head_end)
        ld.start(); ld.wait()
    x = x_ref[0]
    for i, b in ((0, 0), (1, None), (2, 1)):
        r = dot(x, w[i * D:(i + 1) * D])
        if b is not None: r = r + vec_ref[b:b + 1]
        qkv_ref[0, :, i * D:(i + 1) * D] = r.astype(bf16)
    length = lens[s]
    lane = lax.broadcasted_iota(jnp.int32, (L, 128), 1)
    low = lane < HD
    valid = lax.broadcasted_iota(jnp.int32, (1, L), 1) < length
    ones = jnp.ones((L, 128), bf16)
    stats = jnp.zeros((L, 128), f32)
    scale = LOG2E * HD ** -0.5
    for p in range(H // 2):
        q2 = qkv_ref[0, :, p * 128:(p + 1) * 128]
        k2 = qkv_ref[0, :, D + p * 128:D + (p + 1) * 128]
        v2 = qkv_ref[0, :, 2 * D + p * 128:2 * D + (p + 1) * 128]
        va = jnp.concatenate([v2, ones], axis=1)
        outs = []
        for h in range(2):
            qm = jnp.where(low if h == 0 else ~low, q2, jnp.zeros_like(q2))
            sc = jnp.where(valid, dot(qm, k2, NT) * scale, MASK_FILL)
            top = jnp.max(sc, axis=1, keepdims=True)
            e = jnp.exp2(sc - top).astype(bf16)
            o = dot(e, va)
            tot = o[:, 128:]
            outs.append(o[:, :128] / tot)
            stats = jnp.where(lane == 2 * p + h, top + jnp.log2(tot), stats)
        ctx_ref[0, :, p * 128:(p + 1) * 128] = jnp.where(low, outs[0], outs[1]).astype(bf16)
    st_ref[0] = stats.T

def attn_fwd(plan, pieces, place, lengths, tokens, vec):
    n = len(pieces); S = tokens.shape[0]
    return pl.pallas_call(
        functools.partial(attn_fwd_kernel, plan, n), grid=(S,), name="attn_fwd",
        in_specs=[SMEM, SMEM, pl.BlockSpec((1, L, D), lambda s: (s, 0, 0)), pl.BlockSpec((16, D), lambda s: (0, 0))] + [HBM] * n,
        out_specs=[pl.BlockSpec((1, L, 3 * D), lambda s: (s, 0, 0)), pl.BlockSpec((1, L, D), lambda s: (s, 0, 0)), pl.BlockSpec((1, 128, L), lambda s: (s, 0, 0))],
        out_shape=[jax.ShapeDtypeStruct((S, L, 3 * D), bf16), jax.ShapeDtypeStruct((S, L, D), bf16), jax.ShapeDtypeStruct((S, 128, L), f32)],
        scratch_shapes=[pltpu.VMEM((plan.head_end, D), bf16), pltpu.SemaphoreType.DMA((len(plan.spans),))],
        compiler_params=pltpu.CompilerParams(vmem_limit_bytes=50 << 20),
        cost_estimate=pl.CostEstimate(flops=8 * 10 ** 9, bytes_accessed=14 * 10 ** 6, transcendentals=6 * 10 ** 6),
    )(place, lengths, tokens, vec, *pieces)

def norm(h):
    mu = jnp.mean(h, axis=1, keepdims=True)
    c = h - mu
    r = lax.rsqrt(jnp.mean(c * c, axis=1, keepdims=True) + LN_EPS)
    return c * r, r

def norm_back(g, xh, r, gain):
    a = g * gain
    return r * (a - jnp.mean(a, axis=1, keepdims=True) - xh * jnp.mean(a * xh, axis=1, keepdims=True))

def gelu_both(u):
    phi = 0.5 + 0.5 * lax.erf(u * 2**-0.5)
    bell = jnp.exp2(u * u * (-0.5 * LOG2E))
    return u * phi, phi + (u * bell) * (2 * math.pi) ** -0.5


def ffn_kernel(plan, layout, n, tiles, low, place, labels, exits, count, cls, x_ref, c_ref, og_ref, vec_ref, *refs):
    m = n + 5 + len(layout.shapes)
    pieces, gw_refs = refs[:n], refs[n + 5:m]
    out_ref, dh1_ref, dc_ref, vg_ref, sc_ref = refs[n:n + 5]
    w, sems, g_s, du_s, n1_s, df_s, da_s, cc_s, gp_s, dy_s, e_s, z_s, osem = refs[m:]
    i = pl.program_id(0)
    ld = Loads(plan, pieces, place, w, sems, low, MROWS)
    @pl.when(i == 0)
    def _():
        ld.start()
        vg_ref[...] = jnp.zeros_like(vg_ref); sc_ref[...] = jnp.zeros_like(sc_ref)
        ld.wait()
    wo, wp, w1, w2 = 3 * D - low, 4 * D - low, 5 * D - low, 5 * D + FF - low
    vrow = lambda r: vec_ref[r:r + 1]
    rows = pl.ds(pl.multiple_of(i * TILE, TILE), TILE)
    c = c_ref[...]
    cc_s[rows] = c
    h1 = x_ref[...].astype(f32) + (dot(c, w[wo:wo + D]) + vrow(2))
    xh1, r1 = norm(h1)
    n1 = xh1 * vrow(3) + vrow(4)
    n1b = n1.astype(bf16)
    n1_s[rows] = n1b
    f = None
    for j in range(0, FF, UNITS):
        bias = jnp.concatenate([vrow(9 + i) for i in range(j // D, (j + UNITS) // D)], axis=1)
        g, gp = gelu_both(dot(n1b, w[w1 + j:w1 + j + UNITS], NT) + bias)
        gb = g.astype(bf16)
        g_s[rows, j:j + UNITS] = gb
        gp_s[:, j:j + UNITS] = gp
        part = dot(gb, w[w2 + j:w2 + j + UNITS])
        f = part if f is None else f + part
    xh2, r2 = norm(n1 + (f + vrow(5)))
    yb = (xh2 * vrow(6) + vrow(7)).astype(bf16)
    out_ref[...] = yb
    dy_s[...] = og_ref[...].astype(f32)
    per = L // TILE
    @pl.when(lax.rem(i, per) == 0)
    def _():
        s = i // per
        head = lax.broadcasted_iota(jnp.int32, (R, 1), 0) == 0
        act = jnp.where(head, jnp.where(exits[s] >= LAYER, 1.0, 0.0), 0.0)
        e8 = jnp.where(head, yb[:R].astype(f32), 0.0).astype(bf16)
        pool = jnp.tanh(dot(e8, w[wp:wp + D]) + vrow(8))
        pb = pool.astype(bf16).astype(f32)
        lg = [jnp.sum(pb * vrow(13 + k), axis=1, keepdims=True) + cls[k] for k in range(NCLS)]
        top = jnp.maximum(jnp.maximum(lg[0], lg[1]), lg[2])
        lse = top + jnp.log(jnp.exp(lg[0] - top) + jnp.exp(lg[1] - top) + jnp.exp(lg[2] - top))
        hot = [jnp.where(labels[s] == k, 1.0, 0.0) for k in range(NCLS)]
        ce = act * (lse - (lg[0] * hot[0] + lg[1] * hot[1] + lg[2] * hot[2]))
        err = [act * (jnp.exp(lg[k] - lse) - hot[k]) for k in range(NCLS)]
        lane = lax.broadcasted_iota(jnp.int32, (R, 128), 1)
        got = jnp.where(lane == 0, ce, 0.0)
        for k in range(NCLS): got = jnp.where(lane == 1 + k, err[k], got)
        sc_ref[...] += got
        dl = [(err[k] / count[0]).astype(bf16).astype(f32) for k in range(NCLS)]
        gpool = dl[0] * vrow(13) + dl[1] * vrow(14) + dl[2] * vrow(15)
        dz = (gpool * (1.0 - pool * pool)).astype(bf16)
        srow = pl.ds(pl.multiple_of(s * R, R), R)
        e_s[srow] = e8; z_s[srow] = dz
        vg_ref[8:9] += jnp.sum(dz.astype(f32), axis=0, keepdims=True)
        for k in range(NCLS): vg_ref[13 + k:14 + k] += jnp.sum(dl[k] * pb, axis=0, keepdims=True)
        dy_s[0:R] += dot(dz, w[wp:wp + D], NT)
    dy = dy_s[...]
    def vsum(r, v): vg_ref[r:r + 1] += jnp.sum(v, axis=0, keepdims=True)
    vsum(6, dy * xh2); vsum(7, dy)
    dh2 = norm_back(dy, xh2, r2, vrow(6))
    dfb = dh2.astype(bf16)
    df_s[rows] = dfb
    vsum(5, dfb.astype(f32))
    dn1 = dh2
    for j in range(0, FF, UNITS):
        du = (dot(dfb, w[w2 + j:w2 + j + UNITS], NT) * gp_s[:, j:j + UNITS]).astype(bf16)
        du_s[rows, j:j + UNITS] = du
        for part_at in range(0, UNITS, D):
            vsum(9 + (part_at + j) // D, du[:, part_at:part_at + D].astype(f32))
        dn1 = dn1 + dot(du, w[w1 + j:w1 + j + UNITS])
    vsum(3, dn1 * xh1); vsum(4, dn1)
    dh1 = norm_back(dn1, xh1, r1, vrow(3))
    dh1_ref[...] = dh1
    dab = dh1.astype(bf16)
    da_s[rows] = dab
    vsum(2, dab.astype(f32))
    dc_ref[...] = dot(dab, w[wo:wo + D], NT).astype(bf16)
    @pl.when(i == tiles - 1)
    def _():
        for lhs, rhs, width, base in ((e_s, z_s, D, 4 * D), (cc_s, da_s, D, 3 * D), (du_s, n1_s, FF, 5 * D), (g_s, df_s, FF, 5 * D + FF)):

            size = min(width, CHUNK)

            def step(r, carry, lhs=lhs, rhs=rhs, base=base, size=size):
                at = pl.multiple_of(r * size, size)
                w[pl.ds(pl.multiple_of(base - low + at, 16), size)] = dot(lhs[:, pl.ds(at, size)], rhs[...], TN).astype(bf16)
                return carry

            lax.fori_loop(0, width // size, step, 0)
            layout.write(place, w, low, gw_refs, osem.at[0], base, width)
        layout.wait(w, low, gw_refs, osem.at[0], 3 * D, MROWS - 3 * D)

def ffn(plan, layout, pieces, place, labels, exits, count, cls, x, ctx, og, vec):
    n = len(pieces); T = x.shape[0]; tiles = T // TILE; low = plan.tail_start
    tok = lambda dt: pl.BlockSpec((TILE, D), lambda i: (i, 0))
    return pl.pallas_call(
        functools.partial(ffn_kernel, plan, layout, n, tiles, low), grid=(tiles,), name="ffn",
        in_specs=[SMEM] * 5 + [tok(0)] * 3 + [pl.BlockSpec((16, D), lambda i: (0, 0))] + [HBM] * n,
        out_specs=[tok(0), tok(0), tok(0), pl.BlockSpec((16, D), lambda i: (0, 0)), pl.BlockSpec((R, 128), lambda i: (0, 0))] + [ANY] * len(layout.shapes),
        out_shape=[jax.ShapeDtypeStruct((T, D), bf16), jax.ShapeDtypeStruct((T, D), f32), jax.ShapeDtypeStruct((T, D), bf16), jax.ShapeDtypeStruct((16, D), f32), jax.ShapeDtypeStruct((R, 128), f32)] + layout.shapes,
        scratch_shapes=[pltpu.VMEM((MROWS - low, D), bf16), pltpu.SemaphoreType.DMA((len(plan.spans),)),
            pltpu.VMEM((T, FF), bf16), pltpu.VMEM((T, FF), bf16), pltpu.VMEM((T, D), bf16), pltpu.VMEM((T, D), bf16), pltpu.VMEM((T, D), bf16), pltpu.VMEM((T, D), bf16),
            pltpu.VMEM((TILE, FF), f32), pltpu.VMEM((TILE, D), f32), pltpu.VMEM((R * (T // L), D), bf16), pltpu.VMEM((R * (T // L), D), bf16),
            pltpu.SemaphoreType.DMA((1,))],
        compiler_params=pltpu.CompilerParams(vmem_limit_bytes=60 << 20),
        cost_estimate=pl.CostEstimate(flops=33 * 10 ** 9, bytes_accessed=40 * 10 ** 6, transcendentals=6 * 10 ** 6),
    )(place, labels, exits, count, cls, x, ctx, og, vec, *pieces)

def attn_bwd_kernel(plan, layout, n, S, place, lens, x_ref, qkv_ref, dc_ref, c_ref, st_ref, dh1_ref, *refs):
    m = len(layout.shapes)
    pieces = refs[:n]
    dx_ref, vg_ref = refs[n + m:n + m + 2]
    gw_refs = refs[n + m + 2:n + 2 * m + 2]
    w, sems, d_s, x_s, osem = refs[n + 2 * m + 2:]
    s = pl.program_id(0)
    ld = Loads(plan, pieces, place, w, sems, 0, plan.head_end)
    @pl.when(s == 0)
    def _():
        ld.start()
        vg_ref[...] = jnp.zeros_like(vg_ref)
    rows = pl.ds(pl.multiple_of(s * L, L), L)
    x_s[rows] = x_ref[0]
    length = lens[s]
    low = lax.broadcasted_iota(jnp.int32, (L, 128), 1) < HD
    zero = jnp.zeros((L, 128), bf16)
    apart = lambda v: jnp.concatenate([jnp.where(low, v, zero), jnp.where(low, zero, v)], axis=0)
    join = lambda v: jnp.where(low, v[:L], v[L:])
    valid = lax.broadcasted_iota(jnp.int32, (L, 1), 0) < length
    scale = LOG2E * HD ** -0.5
    at = lambda i, p: slice(i * D + p * 128, i * D + (p + 1) * 128)

    def scores(p):
        q2, k2, v2 = (qkv_ref[0, :, at(i, p)] for i in range(3))
        ks, dc2 = apart(k2), dc_ref[0, :, at(0, p)]
        return ks, q2, dc2, dot(ks, q2, NT), dot(apart(v2), dc2, NT)

    ahead = scores(0)
    for p in range(H // 2):
        ks, q2, dc2, score, dprob = ahead
        if p + 1 < H // 2:
            ahead = scores(p + 1)
        prod = (dc2.astype(f32) * c_ref[0, :, at(0, p)].astype(f32)).T
        probs, dscores = [], []
        for h in range(2):
            delta = jnp.sum(prod[h * HD:(h + 1) * HD], axis=0, keepdims=True)
            rows_h = slice(h * L, (h + 1) * L)
            st = jnp.where(valid, score[rows_h] * scale, MASK_FILL)
            pt = jnp.exp2(st - st_ref[0, 2 * p + h:2 * p + h + 1, :])
            probs.append(pt.astype(bf16))
            dscores.append((pt * (dprob[rows_h] - delta)).astype(bf16))
        dst = jnp.concatenate(dscores, axis=0)
        d_s[rows, at(0, p)] = (dot(dst, ks, TN) * HD ** -0.5).astype(bf16)
        d_s[rows, at(1, p)] = (join(dot(dst, q2)) * HD ** -0.5).astype(bf16)
        d_s[rows, at(2, p)] = join(dot(jnp.concatenate(probs, axis=0), dc2)).astype(bf16)
    @pl.when(s == 0)
    def _(): ld.wait()
    dq, dk, dv = (d_s[rows, i * D:(i + 1) * D] for i in range(3))
    dx_ref[0] = (dh1_ref[0] + dot(dq, w[0:D], NT) + dot(dk, w[D:2 * D], NT) + dot(dv, w[2 * D:3 * D], NT)).astype(bf16)
    vg_ref[0:1] += jnp.sum(dq.astype(f32), axis=0, keepdims=True)
    vg_ref[1:2] += jnp.sum(dv.astype(f32), axis=0, keepdims=True)
    @pl.when(s == S - 1)
    def _():
        for i in range(3):
            w[i * D:(i + 1) * D] = dot(x_s[...], d_s[:, i * D:(i + 1) * D], TN).astype(bf16)
            layout.write(place, w, 0, gw_refs, osem.at[0], i * D, D)
        layout.wait(w, 0, gw_refs, osem.at[0], 0, 3 * D)

def attn_bwd(plan, layout, pieces, place, lengths, tokens, qkv, dc, ctx, st, dh1, gw):
    n, m, S = len(pieces), len(gw), tokens.shape[0]
    seq = lambda *sh: pl.BlockSpec((1,) + sh, lambda s: (s, 0, 0))
    return pl.pallas_call(
        functools.partial(attn_bwd_kernel, plan, layout, n, S), grid=(S,), name="attn_bwd",
        in_specs=[SMEM, SMEM, seq(L, D), seq(L, 3 * D), seq(L, D), seq(L, D), seq(128, L), seq(L, D)] + [HBM] * n + [ANY] * m,
        out_specs=[seq(L, D), pl.BlockSpec((8, D), lambda s: (0, 0))] + [ANY] * m,
        out_shape=[jax.ShapeDtypeStruct((S, L, D), bf16), jax.ShapeDtypeStruct((8, D), f32)] + layout.shapes,
        input_output_aliases={8 + n + i: 2 + i for i in range(m)},
        scratch_shapes=[pltpu.VMEM((plan.head_end, D), bf16), pltpu.SemaphoreType.DMA((len(plan.spans),)), pltpu.VMEM((S * L, 3 * D), bf16), pltpu.VMEM((S * L, D), bf16), pltpu.SemaphoreType.DMA((1,))],
        compiler_params=pltpu.CompilerParams(vmem_limit_bytes=56 << 20),
        cost_estimate=pl.CostEstimate(flops=16 * 10 ** 9, bytes_accessed=24 * 10 ** 6, transcendentals=6 * 10 ** 6),
    )(place, lengths, tokens, qkv, dc, ctx, st, dh1, *pieces, *gw)


FSDP = 16


WAYS = {
    "x": ("fsdp", tuple((i, i ^ 2) for i in range(FSDP))),
    "y": ("dp", ((0, 1), (1, 0))),
    "z": ("fsdp", tuple((i, (i + 4) % FSDP) for i in range(FSDP))),
    "core": ("fsdp", tuple((i, i ^ 1) for i in range(FSDP))),
}
PARTS = (80, 128, 144)
HALF = 160


def hold(value, *others):
    return lax.optimization_barrier((value, *others))[0] if others else value


def send(way, *values):
    return lax.ppermute(values[0] if len(values) == 1 else jnp.concatenate(values), *WAYS[way])


def position():
    index = lax.axis_index("fsdp")
    return index // 4, index // 2 % 2, index % 2, lax.axis_index("dp")


def gather(shard, small):
    a, c, e = PARTS
    rows, rep = shard.shape[0], lax.axis_index("dp")
    cut = lax.dynamic_slice_in_dim
    all_a, all_e = shard[:a], shard[a + 2 * c :]
    my_c, my_e = cut(shard, a + rep * c, c), cut(shard, a + 2 * c + rep * e, e)
    late = 2 * e - EARLY
    zc, ze = (lambda k: z[k][:c]), (lambda k: z[k][c : c + e])
    z, za = {}, {}
    z[1] = send("z", my_c, my_e, small)
    x1 = send("x", all_a, my_c, all_e[:EARLY])
    z[2] = send("z", z[1])
    x2 = send("x", all_e[EARLY:], zc(1))
    y2 = send("y", x1[a : a + c], ze(1))
    za[1] = send("z", all_a, x1[:a])
    x3 = send("x", zc(2), ze(1), y2[c:])
    y3 = send("y", zc(1), x2[late:], ze(2))
    z[3] = send("z", hold(z[2], x2))
    za[2] = send("z", hold(za[1], y2, x2))
    small = small + z[1][c + e :] + z[2][c + e :] + z[3][c + e :]
    x4 = send("x", zc(3), ze(2), y3[2 * c :], small)
    y4 = send("y", zc(2), x3[:c], ze(3))
    za[3] = send("z", hold(za[2], y3, x3))
    small = small + x4[c + 2 * e :]
    x5 = send("x", ze(3), y4[2 * c :])
    y5 = send("y", zc(3), x4[:c], small)
    small = small + y5[2 * c :]
    za = {1: hold(za[1], x3, y3), 2: hold(za[2], x4, y4), 3: hold(za[3], x5, y5)}
    small = small + send("core", small)
    held = [(shard, ((0, rows, 0, 0, "all"),))]
    for k in (1, 2, 3):
        held.append((z[k], ((0, c, k, 0, "c_mine"), (c, e, k, 0, "e_mine"))))
        held.append((za[k], ((0, a, k, 0, "a"), (a, a, k, 1, "a"))))
    held.append((x1, ((0, a, 0, 1, "a"), (a, c, 0, 1, "c_mine"), (a + c, EARLY, 0, 1, "e"))))
    held.append((x2, ((0, late, 0, 1, "e_late"), (late, c, 1, 1, "c_mine"))))
    held.append((y2, ((0, c, 0, 1, "c_other"), (c, e, 1, 0, "e_other"))))
    for k, x_got, y_got in ((2, x3, y3), (3, x4, y4)):
        held.append((x_got, ((0, c, k, 1, "c_mine"), (c, e, k - 1, 1, "e_mine"), (c + e, e, k - 1, 1, "e_other"))))
        held.append((y_got, ((0, c, k - 1, 0, "c_other"), (c, c, k - 1, 1, "c_other"), (2 * c, e, k, 0, "e_other"))))
    held.append((x5, ((0, e, 3, 1, "e_mine"), (e, e, 3, 1, "e_other"))))
    held.append((y5, ((0, c, 3, 0, "c_other"), (c, c, 3, 1, "c_other"))))
    pieces, plan = [], Plan([], rows, PARTS)
    for value, parts in held:
        for other_core, piece in ((0, value), (1, send("core", value))):
            for start, count, steps, other_x, part in parts:
                plan.spans.append((len(pieces), start, count, (steps, other_x, other_core, part)))
            pieces.append(piece)
    return pieces, plan, small


def add_low(a, b):
    return (a.astype(f32) + b.astype(f32)).astype(bf16)


def scatter_sum(grads, small, sums, half):
    rows = grads[0].shape[0] // 2
    c, e = half, rows // 2 - half
    rep = lax.axis_index("dp")
    cut = lax.dynamic_slice_in_dim
    links = {"x": [], "y": [], "z": []}

    def link(name, *values):
        done = links[name]
        first = hold(values[0], *done[-2:-1])
        done.append(send(name, first, *values[1:]))
        return done[-1]

    def packed():
        high = sums.astype(bf16)
        low = (sums - high.astype(f32)).astype(bf16)
        return jnp.concatenate([small, jnp.stack([high, low] + [jnp.zeros_like(high)] * 6)])

    def added(others):
        total, total_sums = small.astype(f32), sums
        for other in others:
            total = total + other[:16].astype(f32)
            total_sums = total_sums + (other[16].astype(f32) + other[17].astype(f32))
        return total.astype(bf16), total_sums

    small, sums = added([send("core", packed())])
    rider, riders = packed(), []
    ring_c = ring_e = to_y = None
    for k in (1, 2, 3, 0):
        keep, got = grads[k], send("core", grads[4 + k])
        part = lambda first, count: add_low(keep[first : first + count], got[first : first + count])
        to_y = part(2 * c, 2 * c)
        yc = link("y", to_y)
        xe = link("x", part(4 * c, 2 * e))
        both_c = add_low(part(0, 2 * c), yc)
        own_e = add_low(part(4 * c + 2 * e, 2 * e), xe)
        if k == 0:
            small, sums = added(riders)
            xc = link("x", both_c[c:], packed())
            small, sums = added([xc[c:]])
        else:
            xc = link("x", both_c[c:])
        ye = link("y", cut(own_e, (1 - rep) * e, e))
        sum_c = both_c[:c].astype(f32) + xc[:c].astype(f32)
        sum_e = cut(own_e, rep * e, e).astype(f32) + ye.astype(f32)
        if ring_c is not None:
            sum_c, sum_e = sum_c + ring_c.astype(f32), sum_e + ring_e[:e].astype(f32)
        sum_c, sum_e = sum_c.astype(bf16), sum_e.astype(bf16)
        if k:
            ring_c, ring_e = link("z", sum_c), link("z", sum_e, rider)
            rider = ring_e[e:]
            riders.append(rider)
    back = send("y", sum_c, sum_e, packed())
    small, sums = added([back[c + e :]])
    order = lambda a, b: [jnp.where(rep == 0, a, b), jnp.where(rep == 0, b, a)]
    return jnp.concatenate(order(sum_c, back[:c]) + order(sum_e, back[c : c + e])), small, sums


def row_rates(row_index):
    base_rate = D ** (-0.5)
    return jnp.where(
        (row_index >= 3 * D) & (row_index < 4 * D),
        8.0 * base_rate,
        jnp.where(row_index >= 5 * D + FF, 1.5 * FF ** (-0.5), base_rate),
    )


def adam_update(master, first_mom, second_mom, grad_in, rate, decay):
    first_new = BETA_ONE * first_mom + (1.0 - BETA_ONE) * grad_in
    second_new = BETA_TWO * second_mom + (1.0 - BETA_TWO) * grad_in * grad_in
    fix_one = 1.0 - BETA_ONE**STEP
    fix_two = 1.0 - BETA_TWO**STEP
    direction = first_new / fix_one / (jnp.sqrt(second_new / fix_two) + ADAM_EPS)
    master_new = master - rate * (direction + decay * master)
    return (master_new, first_new, second_new)


def on_device(
    paths,
    tokens,
    out_grad,
    lengths,
    labels,
    exit_layers,
    mat_master,
    mat_first,
    mat_second,
    vec_master,
    vec_first,
    vec_second,
    cls_bias,
    cls_first,
    cls_second,
):
    seqs, toks = tokens.shape[0], tokens.shape[0] * L
    shard_rows, lanes = mat_master.shape[0], vec_master.shape[1]
    index = lax.axis_index("fsdp")
    place = jnp.stack(position()).astype(jnp.int32)
    active = jnp.sum((exit_layers >= LAYER).astype(f32))
    mat_low, vec_low = mat_master.astype(bf16), vec_master.astype(bf16)
    if paths:
        placed = lax.dynamic_update_slice(jnp.zeros((16, D), bf16), vec_low, (0, lanes * index))
        placed = jnp.where(lax.axis_index("dp") == 0, placed, jnp.zeros_like(placed))
        layout = Layout(shard_rows, HALF)
        pieces, plan, small = gather(mat_low, jnp.concatenate([placed, jnp.full((8, D), active).astype(bf16)]))
        vectors, active_count = small[:16].astype(f32), small[16, 0].astype(f32)
    else:
        pieces = [lax.all_gather(mat_low, "fsdp", axis=0, tiled=True)]
        plan, layout = Plan([(0, 0, MROWS, 0)], 3 * D), Layout(shard_rows, 0)
        vectors = lax.all_gather(vec_low, "fsdp", axis=1, tiled=True).astype(f32)
        active_count = lax.psum(active, ("dp", "fsdp"))
    qkv, context, stats = attn_fwd(plan, pieces, place, lengths, tokens, vectors)
    block_out, grad_attn, grad_ctx, vec_grad, sums, *mat_grad = ffn(
        plan,
        layout,
        pieces,
        place,
        labels,
        exit_layers,
        active_count.reshape(1),
        cls_bias,
        tokens.reshape(toks, D),
        context.reshape(toks, D),
        out_grad.reshape(toks, D),
        vectors,
    )
    input_grad, head_grad, *mat_grad = attn_bwd(
        plan,
        layout,
        pieces,
        place,
        lengths,
        tokens,
        qkv,
        grad_ctx.reshape(seqs, L, D),
        context,
        stats,
        grad_attn.reshape(seqs, L, D),
        mat_grad,
    )
    vec_grad = jnp.concatenate([head_grad[:2], vec_grad[2:]])
    sums = jnp.sum(sums, axis=0)
    if paths:
        mat_total, vec_total, sums = scatter_sum(mat_grad, vec_grad.astype(bf16), jnp.pad(sums, (0, D - 128)), HALF)
        mat_total = mat_total.astype(f32)
        vec_total = lax.dynamic_slice(vec_total, (0, lanes * index), (16, lanes)).astype(f32)
    else:
        part = lax.psum_scatter(mat_grad[0], "fsdp", scatter_dimension=0, tiled=True)
        mat_total = lax.psum(part, "dp").astype(f32)
        part = lax.psum_scatter(vec_grad.astype(bf16), "fsdp", scatter_dimension=1, tiled=True)
        vec_total = lax.psum(part, "dp").astype(f32)
        sums = lax.psum(sums[:4], ("dp", "fsdp"))
    ramp_loss = sums[0] / active_count
    cls_grad = sums[1:4] / active_count
    rates = row_rates(index * shard_rows + jnp.arange(shard_rows))[:, None]
    mat_new, mat_first_new, mat_second_new = adam_update(
        mat_master, mat_first, mat_second, mat_total, rates, WEIGHT_DECAY
    )
    vec_new, vec_first_new, vec_second_new = adam_update(
        vec_master, vec_first, vec_second, vec_total, VEC_RATE, 0.0
    )
    cls_new, cls_first_new, cls_second_new = adam_update(
        cls_bias, cls_first, cls_second, cls_grad, VEC_RATE, 0.0
    )
    return (
        block_out.reshape(seqs, L, D),
        input_grad,
        ramp_loss,
        mat_new,
        mat_first_new,
        mat_second_new,
        mat_new.astype(bf16),
        vec_new,
        vec_first_new,
        vec_second_new,
        vec_new.astype(bf16),
        cls_new,
        cls_first_new,
        cls_second_new,
    )


def solution(mesh):
    rows = P(("dp", "fsdp"), None, None)
    each = P(("dp", "fsdp"))
    mat, vec = P("fsdp", None), P(None, "fsdp")
    paths = (mesh.shape["dp"], mesh.shape["fsdp"]) == (2, FSDP)
    return jax.shard_map(
        functools.partial(on_device, paths),
        mesh=mesh,
        in_specs=(rows, rows, each, each, each, mat, mat, mat, vec, vec, vec, P(), P(), P()),
        out_specs=(rows, rows, P(), mat, mat, mat, mat, vec, vec, vec, vec, P(), P(), P()),
        check_vma=False,
    )
```

```python
import functools
import math

import jax
import jax.numpy as jnp
from jax import lax
from jax.experimental import pallas as pl
from jax.experimental.pallas import tpu as pltpu
from jax.sharding import PartitionSpec as P

D, H, HD, FF, NCLS, L = 768, 12, 64, 3072, 3, 512
LAYER = 6
STEP = 10
BETA_ONE = 0.9
BETA_TWO = 0.999
ADAM_EPS = 1e-08
WEIGHT_DECAY = 0.01
VEC_RATE = 0.5
LN_EPS = 1e-12
MASK_FILL = -1e9
LOG2E = 1.4426950408889634
f32, bf16 = jnp.float32, jnp.bfloat16
NN = (((1,), (0,)), ((), ()))
NT = (((1,), (1,)), ((), ()))
TN = (((0,), (0,)), ((), ()))
def dot(a, b, dims=NN):
    return lax.dot_general(a, b, dims, preferred_element_type=f32)
ANY = pl.BlockSpec(memory_space=pl.ANY)
VMEM = pl.BlockSpec(memory_space=pltpu.VMEM)
HBM = pl.BlockSpec(memory_space=pltpu.HBM)
MROWS = 5 * D + 2 * FF
EARLY = 128
CHUNK = 1536
UNITS = 1536
SMEM = pl.BlockSpec(memory_space=pltpu.SMEM)
TILE = 256
R = 16


class Loads:
    def __init__(self, plan, refs, place, dst, sems, low, high):
        self.items = []
        for j, (piece, src, count, row) in enumerate(plan.spans):
            if isinstance(row, int):
                first, last = max(row, low), min(row + count, high)
                if first >= last:
                    continue
                cond = None
                source = refs[piece].at[pl.ds(src + first - row, last - first)]
                target = dst.at[pl.ds(first - low, last - first)]
            else:
                shard, at = plan.locate(row, place)
                cond = (shard * plan.rows >= low) & (shard * plan.rows < high)
                source = refs[piece].at[pl.ds(src, count)]
                target = dst.at[pl.ds(pl.multiple_of(jnp.where(cond, at - low, 0), 16), count)]
            self.items.append((cond, pltpu.make_async_copy(source, target, sems.at[j])))

    def start(self):
        for cond, copy in self.items:
            if cond is None:
                copy.start()
            else:
                pl.when(cond)(copy.start)

    def wait(self):
        for cond, copy in self.items:
            if cond is None:
                copy.wait()
            else:
                pl.when(cond)(copy.wait)


class Plan:
    def __init__(self, spans, rows, parts=(0, 0, 0)):
        self.spans, self.rows, self.parts = spans, rows, parts
        self.head_end = -(-3 * D // rows) * rows
        self.tail_start = 3 * D // rows * rows

    def locate(self, where, place):
        steps, other_x, other_core, part = where
        z, x, core, rep = (place[i] for i in range(4))
        flip = lambda bit, other: 1 - bit if other else bit
        shard = (lax.rem(z - steps + 4, 4) * 2 + flip(x, other_x)) * 2 + flip(core, other_core)
        a, c, e = self.parts
        base = {
            "all": 0,
            "a": 0,
            "c_mine": a + rep * c,
            "c_other": a + (1 - rep) * c,
            "e": a + 2 * c,
            "e_late": a + 2 * c + EARLY,
            "e_mine": a + 2 * c + rep * e,
            "e_other": a + 2 * c + (1 - rep) * e,
        }[part]
        return shard, shard * self.rows + base


class Layout:
    def __init__(self, rows, half):
        self.rows, self.half = rows, half
        self.shapes = [jax.ShapeDtypeStruct((2 * rows, D), bf16)] * 8 if half else [jax.ShapeDtypeStruct((MROWS, D), bf16)]

    def write(self, place, staged, low, targets, sem, first, count):
        def start(target, at, rows, row):
            pltpu.make_async_copy(staged.at[pl.ds(at - low, rows)], target.at[pl.ds(row, rows)], sem).start()

        if not self.half:
            start(targets[0], first, count, first)
            return
        z, x, core, rep = (place[i] for i in range(4))
        rows, half = self.rows, self.half
        for shard in range(first // rows, -(-(first + count) // rows)):
            far_x, far_core = jnp.abs(x - shard // 2 % 2), jnp.abs(core - shard % 2)
            group = far_core * 4 + lax.rem(z - shard // 4 + 4, 4)
            runs = (
                (0, half, rep * 2 * half + far_x * half),
                (half, half, (1 - rep) * 2 * half + far_x * half),
                (2 * half, rows - 2 * half, 4 * half + (1 - far_x) * (rows - 2 * half)),
            )

            def put(target, shard=shard, runs=runs):
                for inner, size, row in runs:
                    begin = max(first, shard * rows + inner)
                    end = min(first + count, shard * rows + inner + size)
                    if begin < end:
                        start(target, begin, end - begin, pl.multiple_of(row + begin - shard * rows - inner, 16))

            for index, target in enumerate(targets):
                pl.when(group == index)(functools.partial(put, target))

    def wait(self, staged, low, targets, sem, first, count):
        rows = staged.at[pl.ds(first - low, count)]
        pltpu.make_async_copy(rows, rows, sem).wait()


def attn_fwd_kernel(plan, n, place, lens, x_ref, vec_ref, *refs):
    pieces = refs[:n]; qkv_ref, ctx_ref, st_ref, w, sems = refs[n:]
    s = pl.program_id(0)
    @pl.when(s == 0)
    def _():
        ld = Loads(plan, pieces, place, w, sems, 0, plan.head_end)
        ld.start(); ld.wait()
    x = x_ref[0]
    for i, b in ((0, 0), (1, None), (2, 1)):
        r = dot(x, w[i * D:(i + 1) * D])
        if b is not None: r = r + vec_ref[b:b + 1]
        qkv_ref[0, :, i * D:(i + 1) * D] = r.astype(bf16)
    length = lens[s]
    lane = lax.broadcasted_iota(jnp.int32, (L, 128), 1)
    low = lane < HD
    valid = lax.broadcasted_iota(jnp.int32, (1, L), 1) < length
    ones = jnp.ones((L, 128), bf16)
    stats = jnp.zeros((L, 128), f32)
    scale = LOG2E * HD ** -0.5
    for p in range(H // 2):
        q2 = qkv_ref[0, :, p * 128:(p + 1) * 128]
        k2 = qkv_ref[0, :, D + p * 128:D + (p + 1) * 128]
        v2 = qkv_ref[0, :, 2 * D + p * 128:2 * D + (p + 1) * 128]
        va = jnp.concatenate([v2, ones], axis=1)
        outs = []
        for h in range(2):
            qm = jnp.where(low if h == 0 else ~low, q2, jnp.zeros_like(q2))
            sc = jnp.where(valid, dot(qm, k2, NT) * scale, MASK_FILL)
            top = jnp.max(sc, axis=1, keepdims=True)
            e = jnp.exp2(sc - top).astype(bf16)
            o = dot(e, va)
            tot = o[:, 128:]
            outs.append(o[:, :128] / tot)
            stats = jnp.where(lane == 2 * p + h, top + jnp.log2(tot), stats)
        ctx_ref[0, :, p * 128:(p + 1) * 128] = jnp.where(low, outs[0], outs[1]).astype(bf16)
    st_ref[0] = stats.T

def attn_fwd(plan, pieces, place, lengths, tokens, vec):
    n = len(pieces); S = tokens.shape[0]
    return pl.pallas_call(
        functools.partial(attn_fwd_kernel, plan, n), grid=(S,), name="attn_fwd",
        in_specs=[SMEM, SMEM, pl.BlockSpec((1, L, D), lambda s: (s, 0, 0)), pl.BlockSpec((16, D), lambda s: (0, 0))] + [HBM] * n,
        out_specs=[pl.BlockSpec((1, L, 3 * D), lambda s: (s, 0, 0)), pl.BlockSpec((1, L, D), lambda s: (s, 0, 0)), pl.BlockSpec((1, 128, L), lambda s: (s, 0, 0))],
        out_shape=[jax.ShapeDtypeStruct((S, L, 3 * D), bf16), jax.ShapeDtypeStruct((S, L, D), bf16), jax.ShapeDtypeStruct((S, 128, L), f32)],
        scratch_shapes=[pltpu.VMEM((plan.head_end, D), bf16), pltpu.SemaphoreType.DMA((len(plan.spans),))],
        compiler_params=pltpu.CompilerParams(vmem_limit_bytes=50 << 20),
        cost_estimate=pl.CostEstimate(flops=8 * 10 ** 9, bytes_accessed=14 * 10 ** 6, transcendentals=6 * 10 ** 6),
    )(place, lengths, tokens, vec, *pieces)

def norm(h):
    mu = jnp.mean(h, axis=1, keepdims=True)
    c = h - mu
    r = lax.rsqrt(jnp.mean(c * c, axis=1, keepdims=True) + LN_EPS)
    return c * r, r

def norm_back(g, xh, r, gain):
    a = g * gain
    return r * (a - jnp.mean(a, axis=1, keepdims=True) - xh * jnp.mean(a * xh, axis=1, keepdims=True))

def gelu_both(u):
    phi = 0.5 + 0.5 * lax.erf(u * 2**-0.5)
    bell = jnp.exp2(u * u * (-0.5 * LOG2E))
    return u * phi, phi + (u * bell) * (2 * math.pi) ** -0.5


def ffn_kernel(plan, layout, n, tiles, low, place, labels, exits, count, cls, x_ref, c_ref, og_ref, vec_ref, *refs):
    m = n + 5 + len(layout.shapes)
    pieces, gw_refs = refs[:n], refs[n + 5:m]
    out_ref, dh1_ref, dc_ref, vg_ref, sc_ref = refs[n:n + 5]
    w, sems, g_s, du_s, n1_s, df_s, da_s, cc_s, gp_s, dy_s, e_s, z_s, osem = refs[m:]
    i = pl.program_id(0)
    ld = Loads(plan, pieces, place, w, sems, low, MROWS)
    @pl.when(i == 0)
    def _():
        ld.start()
        vg_ref[...] = jnp.zeros_like(vg_ref); sc_ref[...] = jnp.zeros_like(sc_ref)
        ld.wait()
    wo, wp, w1, w2 = 3 * D - low, 4 * D - low, 5 * D - low, 5 * D + FF - low
    vrow = lambda r: vec_ref[r:r + 1]
    rows = pl.ds(pl.multiple_of(i * TILE, TILE), TILE)
    c = c_ref[...]
    cc_s[rows] = c
    h1 = x_ref[...].astype(f32) + (dot(c, w[wo:wo + D]) + vrow(2))
    xh1, r1 = norm(h1)
    n1 = xh1 * vrow(3) + vrow(4)
    n1b = n1.astype(bf16)
    n1_s[rows] = n1b
    f = None
    for j in range(0, FF, UNITS):
        bias = jnp.concatenate([vrow(9 + i) for i in range(j // D, (j + UNITS) // D)], axis=1)
        g, gp = gelu_both(dot(n1b, w[w1 + j:w1 + j + UNITS], NT) + bias)
        gb = g.astype(bf16)
        g_s[rows, j:j + UNITS] = gb
        gp_s[:, j:j + UNITS] = gp
        part = dot(gb, w[w2 + j:w2 + j + UNITS])
        f = part if f is None else f + part
    xh2, r2 = norm(n1 + (f + vrow(5)))
    yb = (xh2 * vrow(6) + vrow(7)).astype(bf16)
    out_ref[...] = yb
    dy_s[...] = og_ref[...].astype(f32)
    per = L // TILE
    @pl.when(lax.rem(i, per) == 0)
    def _():
        s = i // per
        head = lax.broadcasted_iota(jnp.int32, (R, 1), 0) == 0
        act = jnp.where(head, jnp.where(exits[s] >= LAYER, 1.0, 0.0), 0.0)
        e8 = jnp.where(head, yb[:R].astype(f32), 0.0).astype(bf16)
        pool = jnp.tanh(dot(e8, w[wp:wp + D]) + vrow(8))
        pb = pool.astype(bf16).astype(f32)
        lg = [jnp.sum(pb * vrow(13 + k), axis=1, keepdims=True) + cls[k] for k in range(NCLS)]
        top = jnp.maximum(jnp.maximum(lg[0], lg[1]), lg[2])
        lse = top + jnp.log(jnp.exp(lg[0] - top) + jnp.exp(lg[1] - top) + jnp.exp(lg[2] - top))
        hot = [jnp.where(labels[s] == k, 1.0, 0.0) for k in range(NCLS)]
        ce = act * (lse - (lg[0] * hot[0] + lg[1] * hot[1] + lg[2] * hot[2]))
        err = [act * (jnp.exp(lg[k] - lse) - hot[k]) for k in range(NCLS)]
        lane = lax.broadcasted_iota(jnp.int32, (R, 128), 1)
        got = jnp.where(lane == 0, ce, 0.0)
        for k in range(NCLS): got = jnp.where(lane == 1 + k, err[k], got)
        sc_ref[...] += got
        dl = [(err[k] / count[0]).astype(bf16).astype(f32) for k in range(NCLS)]
        gpool = dl[0] * vrow(13) + dl[1] * vrow(14) + dl[2] * vrow(15)
        dz = (gpool * (1.0 - pool * pool)).astype(bf16)
        srow = pl.ds(pl.multiple_of(s * R, R), R)
        e_s[srow] = e8; z_s[srow] = dz
        vg_ref[8:9] += jnp.sum(dz.astype(f32), axis=0, keepdims=True)
        for k in range(NCLS): vg_ref[13 + k:14 + k] += jnp.sum(dl[k] * pb, axis=0, keepdims=True)
        dy_s[0:R] += dot(dz, w[wp:wp + D], NT)
    dy = dy_s[...]
    def vsum(r, v): vg_ref[r:r + 1] += jnp.sum(v, axis=0, keepdims=True)
    vsum(6, dy * xh2); vsum(7, dy)
    dh2 = norm_back(dy, xh2, r2, vrow(6))
    dfb = dh2.astype(bf16)
    df_s[rows] = dfb
    vsum(5, dfb.astype(f32))
    dn1 = dh2
    for j in range(0, FF, UNITS):
        du = (dot(dfb, w[w2 + j:w2 + j + UNITS], NT) * gp_s[:, j:j + UNITS]).astype(bf16)
        du_s[rows, j:j + UNITS] = du
        for part_at in range(0, UNITS, D):
            vsum(9 + (part_at + j) // D, du[:, part_at:part_at + D].astype(f32))
        dn1 = dn1 + dot(du, w[w1 + j:w1 + j + UNITS])
    vsum(3, dn1 * xh1); vsum(4, dn1)
    dh1 = norm_back(dn1, xh1, r1, vrow(3))
    dh1_ref[...] = dh1
    dab = dh1.astype(bf16)
    da_s[rows] = dab
    vsum(2, dab.astype(f32))
    dc_ref[...] = dot(dab, w[wo:wo + D], NT).astype(bf16)
    @pl.when(i == tiles - 1)
    def _():
        for lhs, rhs, width, base in ((e_s, z_s, D, 4 * D), (cc_s, da_s, D, 3 * D), (du_s, n1_s, FF, 5 * D), (g_s, df_s, FF, 5 * D + FF)):

            size = min(width, CHUNK)

            def step(r, carry, lhs=lhs, rhs=rhs, base=base, size=size):
                at = pl.multiple_of(r * size, size)
                w[pl.ds(pl.multiple_of(base - low + at, 16), size)] = dot(lhs[:, pl.ds(at, size)], rhs[...], TN).astype(bf16)
                return carry

            lax.fori_loop(0, width // size, step, 0)
            layout.write(place, w, low, gw_refs, osem.at[0], base, width)
        layout.wait(w, low, gw_refs, osem.at[0], 3 * D, MROWS - 3 * D)

def ffn(plan, layout, pieces, place, labels, exits, count, cls, x, ctx, og, vec):
    n = len(pieces); T = x.shape[0]; tiles = T // TILE; low = plan.tail_start
    tok = lambda dt: pl.BlockSpec((TILE, D), lambda i: (i, 0))
    return pl.pallas_call(
        functools.partial(ffn_kernel, plan, layout, n, tiles, low), grid=(tiles,), name="ffn",
        in_specs=[SMEM] * 5 + [tok(0)] * 3 + [pl.BlockSpec((16, D), lambda i: (0, 0))] + [HBM] * n,
        out_specs=[tok(0), tok(0), tok(0), pl.BlockSpec((16, D), lambda i: (0, 0)), pl.BlockSpec((R, 128), lambda i: (0, 0))] + [ANY] * len(layout.shapes),
        out_shape=[jax.ShapeDtypeStruct((T, D), bf16), jax.ShapeDtypeStruct((T, D), f32), jax.ShapeDtypeStruct((T, D), bf16), jax.ShapeDtypeStruct((16, D), f32), jax.ShapeDtypeStruct((R, 128), f32)] + layout.shapes,
        scratch_shapes=[pltpu.VMEM((MROWS - low, D), bf16), pltpu.SemaphoreType.DMA((len(plan.spans),)),
            pltpu.VMEM((T, FF), bf16), pltpu.VMEM((T, FF), bf16), pltpu.VMEM((T, D), bf16), pltpu.VMEM((T, D), bf16), pltpu.VMEM((T, D), bf16), pltpu.VMEM((T, D), bf16),
            pltpu.VMEM((TILE, FF), f32), pltpu.VMEM((TILE, D), f32), pltpu.VMEM((R * (T // L), D), bf16), pltpu.VMEM((R * (T // L), D), bf16),
            pltpu.SemaphoreType.DMA((1,))],
        compiler_params=pltpu.CompilerParams(vmem_limit_bytes=60 << 20),
        cost_estimate=pl.CostEstimate(flops=33 * 10 ** 9, bytes_accessed=40 * 10 ** 6, transcendentals=6 * 10 ** 6),
    )(place, labels, exits, count, cls, x, ctx, og, vec, *pieces)

def attn_bwd_kernel(plan, layout, n, S, place, lens, x_ref, qkv_ref, dc_ref, c_ref, st_ref, dh1_ref, *refs):
    m = len(layout.shapes)
    pieces = refs[:n]
    dx_ref, vg_ref = refs[n + m:n + m + 2]
    gw_refs = refs[n + m + 2:n + 2 * m + 2]
    w, sems, d_s, x_s, osem = refs[n + 2 * m + 2:]
    s = pl.program_id(0)
    ld = Loads(plan, pieces, place, w, sems, 0, plan.head_end)
    @pl.when(s == 0)
    def _():
        ld.start()
        vg_ref[...] = jnp.zeros_like(vg_ref)
    rows = pl.ds(pl.multiple_of(s * L, L), L)
    x_s[rows] = x_ref[0]
    length = lens[s]
    low = lax.broadcasted_iota(jnp.int32, (L, 128), 1) < HD
    zero = jnp.zeros((L, 128), bf16)
    apart = lambda v: jnp.concatenate([jnp.where(low, v, zero), jnp.where(low, zero, v)], axis=0)
    join = lambda v: jnp.where(low, v[:L], v[L:])
    valid = lax.broadcasted_iota(jnp.int32, (L, 1), 0) < length
    scale = LOG2E * HD ** -0.5
    at = lambda i, p: slice(i * D + p * 128, i * D + (p + 1) * 128)

    def scores(p):
        q2, k2, v2 = (qkv_ref[0, :, at(i, p)] for i in range(3))
        ks, dc2 = apart(k2), dc_ref[0, :, at(0, p)]
        return ks, q2, dc2, dot(ks, q2, NT), dot(apart(v2), dc2, NT)

    ahead = scores(0)
    for p in range(H // 2):
        ks, q2, dc2, score, dprob = ahead
        if p + 1 < H // 2:
            ahead = scores(p + 1)
        prod = (dc2.astype(f32) * c_ref[0, :, at(0, p)].astype(f32)).T
        probs, dscores = [], []
        for h in range(2):
            delta = jnp.sum(prod[h * HD:(h + 1) * HD], axis=0, keepdims=True)
            rows_h = slice(h * L, (h + 1) * L)
            st = jnp.where(valid, score[rows_h] * scale, MASK_FILL)
            pt = jnp.exp2(st - st_ref[0, 2 * p + h:2 * p + h + 1, :])
            probs.append(pt.astype(bf16))
            dscores.append((pt * (dprob[rows_h] - delta)).astype(bf16))
        dst = jnp.concatenate(dscores, axis=0)
        d_s[rows, at(0, p)] = (dot(dst, ks, TN) * HD ** -0.5).astype(bf16)
        d_s[rows, at(1, p)] = (join(dot(dst, q2)) * HD ** -0.5).astype(bf16)
        d_s[rows, at(2, p)] = join(dot(jnp.concatenate(probs, axis=0), dc2)).astype(bf16)
    @pl.when(s == 0)
    def _(): ld.wait()
    dq, dk, dv = (d_s[rows, i * D:(i + 1) * D] for i in range(3))
    dx_ref[0] = (dh1_ref[0] + dot(dq, w[0:D], NT) + dot(dk, w[D:2 * D], NT) + dot(dv, w[2 * D:3 * D], NT)).astype(bf16)
    vg_ref[0:1] += jnp.sum(dq.astype(f32), axis=0, keepdims=True)
    vg_ref[1:2] += jnp.sum(dv.astype(f32), axis=0, keepdims=True)
    @pl.when(s == S - 1)
    def _():
        for i in range(3):
            w[i * D:(i + 1) * D] = dot(x_s[...], d_s[:, i * D:(i + 1) * D], TN).astype(bf16)
            layout.write(place, w, 0, gw_refs, osem.at[0], i * D, D)
        layout.wait(w, 0, gw_refs, osem.at[0], 0, 3 * D)

def attn_bwd(plan, layout, pieces, place, lengths, tokens, qkv, dc, ctx, st, dh1, gw):
    n, m, S = len(pieces), len(gw), tokens.shape[0]
    seq = lambda *sh: pl.BlockSpec((1,) + sh, lambda s: (s, 0, 0))
    return pl.pallas_call(
        functools.partial(attn_bwd_kernel, plan, layout, n, S), grid=(S,), name="attn_bwd",
        in_specs=[SMEM, SMEM, seq(L, D), seq(L, 3 * D), seq(L, D), seq(L, D), seq(128, L), seq(L, D)] + [HBM] * n + [ANY] * m,
        out_specs=[seq(L, D), pl.BlockSpec((8, D), lambda s: (0, 0))] + [ANY] * m,
        out_shape=[jax.ShapeDtypeStruct((S, L, D), bf16), jax.ShapeDtypeStruct((8, D), f32)] + layout.shapes,
        input_output_aliases={8 + n + i: 2 + i for i in range(m)},
        scratch_shapes=[pltpu.VMEM((plan.head_end, D), bf16), pltpu.SemaphoreType.DMA((len(plan.spans),)), pltpu.VMEM((S * L, 3 * D), bf16), pltpu.VMEM((S * L, D), bf16), pltpu.SemaphoreType.DMA((1,))],
        compiler_params=pltpu.CompilerParams(vmem_limit_bytes=56 << 20),
        cost_estimate=pl.CostEstimate(flops=16 * 10 ** 9, bytes_accessed=24 * 10 ** 6, transcendentals=6 * 10 ** 6),
    )(place, lengths, tokens, qkv, dc, ctx, st, dh1, *pieces, *gw)


FSDP = 16


WAYS = {
    "x": ("fsdp", tuple((i, i ^ 2) for i in range(FSDP))),
    "y": ("dp", ((0, 1), (1, 0))),
    "z": ("fsdp", tuple((i, (i + 4) % FSDP) for i in range(FSDP))),
    "core": ("fsdp", tuple((i, i ^ 1) for i in range(FSDP))),
}
PARTS = (80, 128, 144)
HALF = 160
BLOCKS = 3


def hold(value, *others):
    return lax.optimization_barrier((value, *others))[0] if others else value


def send(way, *values):
    return lax.ppermute(values[0] if len(values) == 1 else jnp.concatenate(values), *WAYS[way])


def position():
    index = lax.axis_index("fsdp")
    return index // 4, index // 2 % 2, index % 2, lax.axis_index("dp")


def gather(shard, small):
    a, c, e = PARTS
    rows, rep = shard.shape[0], lax.axis_index("dp")
    cut = lax.dynamic_slice_in_dim
    all_a, all_e = shard[:a], shard[a + 2 * c :]
    my_c, my_e = cut(shard, a + rep * c, c), cut(shard, a + 2 * c + rep * e, e)
    late = 2 * e - EARLY
    zc, ze = (lambda k: z[k][:c]), (lambda k: z[k][c : c + e])
    z, za = {}, {}
    z[1] = send("z", my_c, my_e, small)
    x1 = send("x", all_a, my_c, all_e[:EARLY])
    z[2] = send("z", z[1])
    x2 = send("x", all_e[EARLY:], zc(1))
    y2 = send("y", x1[a : a + c], ze(1))
    za[1] = send("z", all_a, x1[:a])
    x3 = send("x", zc(2), ze(1), y2[c:])
    y3 = send("y", zc(1), x2[late:], ze(2))
    z[3] = send("z", hold(z[2], x2))
    za[2] = send("z", hold(za[1], y2, x2))
    small = small + z[1][c + e :] + z[2][c + e :] + z[3][c + e :]
    x4 = send("x", zc(3), ze(2), y3[2 * c :], small)
    y4 = send("y", zc(2), x3[:c], ze(3))
    za[3] = send("z", hold(za[2], y3, x3))
    small = small + x4[c + 2 * e :]
    x5 = send("x", ze(3), y4[2 * c :])
    y5 = send("y", zc(3), x4[:c], small)
    small = small + y5[2 * c :]
    za = {1: hold(za[1], x3, y3), 2: hold(za[2], x4, y4), 3: hold(za[3], x5, y5)}
    small = small + send("core", small)
    held = [(shard, ((0, rows, 0, 0, "all"),))]
    for k in (1, 2, 3):
        held.append((z[k], ((0, c, k, 0, "c_mine"), (c, e, k, 0, "e_mine"))))
        held.append((za[k], ((0, a, k, 0, "a"), (a, a, k, 1, "a"))))
    held.append((x1, ((0, a, 0, 1, "a"), (a, c, 0, 1, "c_mine"), (a + c, EARLY, 0, 1, "e"))))
    held.append((x2, ((0, late, 0, 1, "e_late"), (late, c, 1, 1, "c_mine"))))
    held.append((y2, ((0, c, 0, 1, "c_other"), (c, e, 1, 0, "e_other"))))
    for k, x_got, y_got in ((2, x3, y3), (3, x4, y4)):
        held.append((x_got, ((0, c, k, 1, "c_mine"), (c, e, k - 1, 1, "e_mine"), (c + e, e, k - 1, 1, "e_other"))))
        held.append((y_got, ((0, c, k - 1, 0, "c_other"), (c, c, k - 1, 1, "c_other"), (2 * c, e, k, 0, "e_other"))))
    held.append((x5, ((0, e, 3, 1, "e_mine"), (e, e, 3, 1, "e_other"))))
    held.append((y5, ((0, c, 3, 0, "c_other"), (c, c, 3, 1, "c_other"))))
    pieces, plan = [], Plan([], rows, PARTS)
    for value, parts in held:
        for other_core, piece in ((0, value), (1, send("core", value))):
            for start, count, steps, other_x, part in parts:
                plan.spans.append((len(pieces), start, count, (steps, other_x, other_core, part)))
            pieces.append(piece)
    return pieces, plan, small


def add_low(a, b):
    return (a.astype(f32) + b.astype(f32)).astype(bf16)


def scatter_sum(grads, small, sums, half):
    rows = grads[0].shape[0] // 2
    c, e = half, rows // 2 - half
    rep = lax.axis_index("dp")
    cut = lax.dynamic_slice_in_dim
    links = {"x": [], "y": [], "z": []}

    def link(name, *values):
        done = links[name]
        first = hold(values[0], *done[-2:-1])
        done.append(send(name, first, *values[1:]))
        return done[-1]

    def packed():
        high = sums.astype(bf16)
        low = (sums - high.astype(f32)).astype(bf16)
        return jnp.concatenate([small, jnp.stack([high, low] + [jnp.zeros_like(high)] * 6)])

    def added(others):
        total, total_sums = small.astype(f32), sums
        for other in others:
            total = total + other[:16].astype(f32)
            total_sums = total_sums + (other[16].astype(f32) + other[17].astype(f32))
        return total.astype(bf16), total_sums

    small, sums = added([send("core", packed())])
    riders = []
    ring_c = ring_e = None
    for k in (1, 2, 3, 0):
        keep, got = grads[k], send("core", grads[4 + k])
        part = lambda first, count: add_low(keep[first : first + count], got[first : first + count])
        along = (lambda: (packed(),)) if k == 1 else tuple
        yc = link("y", part(2 * c, 2 * c), *along())
        xe = link("x", part(4 * c, 2 * e))
        both_c = add_low(part(0, 2 * c), yc[: 2 * c])
        own_e = add_low(part(4 * c + 2 * e, 2 * e), xe)
        if k == 1:
            small, sums = added([yc[2 * c :]])
        xc = link("x", both_c[c:], *along())
        if k == 1:
            small, sums = added([xc[c:]])
            riders.append(packed())
        ye = link("y", cut(own_e, (1 - rep) * e, e))
        sum_c = both_c[:c].astype(f32) + xc[:c].astype(f32)
        sum_e = cut(own_e, rep * e, e).astype(f32) + ye.astype(f32)
        if ring_c is not None:
            sum_c, sum_e = sum_c + ring_c.astype(f32), sum_e + ring_e[:e].astype(f32)
        sum_c, sum_e = sum_c.astype(bf16), sum_e.astype(bf16)
        if k:
            ring_c, ring_e = link("z", sum_c), link("z", sum_e, riders[-1])
            riders.append(ring_e[e:])
    small, sums = added(riders[1:])
    mine = jnp.concatenate([sum_c, sum_e])
    return mine, send("y", mine), small, sums


def stage_kernel(after, *refs):
    copies = [pltpu.make_async_copy(refs[i], refs[3 + i], refs[6].at[i]) for i in range(3)]
    for copy in copies:
        copy.start()
    for copy in copies:
        copy.wait()


def update_kernel(half, place, mine, other, master, first, second, *refs):
    targets, (grad, *values), sems = refs[:4], refs[4:9], refs[9]
    c, rows = half, grad.shape[0]
    e, count = rows // 2 - half, rows // BLOCKS
    rep = place[3]
    for start, size, at in ((0, c, 0), (c, e, 2 * c)):
        ours, theirs = mine[start : start + size].astype(f32), other[start : start + size].astype(f32)
        grad[at : at + size] = jnp.where(rep == 0, ours, theirs)
        grad[at + size : at + 2 * size] = jnp.where(rep == 0, theirs, ours)
    shard = (place[0] * 2 + place[1]) * 2 + place[2]
    copies = []
    for block in range(BLOCKS):
        at = pl.ds(block * count, count)
        row = shard * rows + block * count + lax.broadcasted_iota(jnp.int32, (count, 1), 0)
        results = adam_update(master[at], first[at], second[at], grad[at], row_rates(row), WEIGHT_DECAY)
        for i, result in enumerate(results + (results[0].astype(bf16),)):
            values[i][at] = result
            copies.append(pltpu.make_async_copy(values[i].at[at], targets[i].at[at], sems.at[block * 4 + i]))
            copies[-1].start()
    for copy in copies:
        copy.wait()


def update(place, mine, other, master, first, second, half):
    rows = master.shape[0]
    staged = pl.pallas_call(
        stage_kernel,
        name="stage",
        in_specs=[ANY] + [HBM] * 3,
        out_specs=[VMEM] * 3,
        out_shape=[pltpu.VMEM((rows, D), f32)] * 3,
        scratch_shapes=[pltpu.SemaphoreType.DMA((3,))],
        compiler_params=pltpu.CompilerParams(vmem_limit_bytes=4 << 20),
        cost_estimate=pl.CostEstimate(flops=10**6, bytes_accessed=6 * 10**6, transcendentals=0),
    )(mine, master, first, second)
    types = (f32, f32, f32, bf16)
    return pl.pallas_call(
        functools.partial(update_kernel, half),
        name="update",
        in_specs=[SMEM] + [VMEM] * 5,
        out_specs=[HBM] * 4,
        out_shape=[jax.ShapeDtypeStruct((rows, D), dtype) for dtype in types],
        scratch_shapes=[pltpu.VMEM((rows, D), dtype) for dtype in (f32, *types)] + [pltpu.SemaphoreType.DMA((4 * BLOCKS,))],
        compiler_params=pltpu.CompilerParams(vmem_limit_bytes=24 << 20),
        cost_estimate=pl.CostEstimate(flops=10**7, bytes_accessed=7 * 10**6, transcendentals=10**6),
    )(place, mine, other, *staged)


def row_rates(row_index):
    base_rate = D ** (-0.5)
    return jnp.where(
        (row_index >= 3 * D) & (row_index < 4 * D),
        8.0 * base_rate,
        jnp.where(row_index >= 5 * D + FF, 1.5 * FF ** (-0.5), base_rate),
    )


def adam_update(master, first_mom, second_mom, grad_in, rate, decay):
    first_new = BETA_ONE * first_mom + (1.0 - BETA_ONE) * grad_in
    second_new = BETA_TWO * second_mom + (1.0 - BETA_TWO) * grad_in * grad_in
    fix_one = 1.0 - BETA_ONE**STEP
    fix_two = 1.0 - BETA_TWO**STEP
    direction = first_new / fix_one / (jnp.sqrt(second_new / fix_two) + ADAM_EPS)
    master_new = master - rate * (direction + decay * master)
    return (master_new, first_new, second_new)


def on_device(
    paths,
    tokens,
    out_grad,
    lengths,
    labels,
    exit_layers,
    mat_master,
    mat_first,
    mat_second,
    vec_master,
    vec_first,
    vec_second,
    cls_bias,
    cls_first,
    cls_second,
):
    seqs, toks = tokens.shape[0], tokens.shape[0] * L
    shard_rows, lanes = mat_master.shape[0], vec_master.shape[1]
    index = lax.axis_index("fsdp")
    place = jnp.stack(position()).astype(jnp.int32)
    active = jnp.sum((exit_layers >= LAYER).astype(f32))
    mat_low, vec_low = mat_master.astype(bf16), vec_master.astype(bf16)
    if paths:
        placed = lax.dynamic_update_slice(jnp.zeros((16, D), bf16), vec_low, (0, lanes * index))
        placed = jnp.where(lax.axis_index("dp") == 0, placed, jnp.zeros_like(placed))
        layout = Layout(shard_rows, HALF)
        pieces, plan, small = gather(mat_low, jnp.concatenate([placed, jnp.full((8, D), active).astype(bf16)]))
        vectors, active_count = small[:16].astype(f32), small[16, 0].astype(f32)
    else:
        pieces = [lax.all_gather(mat_low, "fsdp", axis=0, tiled=True)]
        plan, layout = Plan([(0, 0, MROWS, 0)], 3 * D), Layout(shard_rows, 0)
        vectors = lax.all_gather(vec_low, "fsdp", axis=1, tiled=True).astype(f32)
        active_count = lax.psum(active, ("dp", "fsdp"))
    qkv, context, stats = attn_fwd(plan, pieces, place, lengths, tokens, vectors)
    block_out, grad_attn, grad_ctx, vec_grad, sums, *mat_grad = ffn(
        plan,
        layout,
        pieces,
        place,
        labels,
        exit_layers,
        active_count.reshape(1),
        cls_bias,
        tokens.reshape(toks, D),
        context.reshape(toks, D),
        out_grad.reshape(toks, D),
        vectors,
    )
    input_grad, head_grad, *mat_grad = attn_bwd(
        plan,
        layout,
        pieces,
        place,
        lengths,
        tokens,
        qkv,
        grad_ctx.reshape(seqs, L, D),
        context,
        stats,
        grad_attn.reshape(seqs, L, D),
        mat_grad,
    )
    vec_grad = jnp.concatenate([head_grad[:2], vec_grad[2:]])
    sums = jnp.sum(sums, axis=0)
    if paths:
        sums = jnp.pad(sums, (0, D - 128))
        mine, other, vec_total, sums = scatter_sum(mat_grad, vec_grad.astype(bf16), sums, HALF)
        vec_total = lax.dynamic_slice(vec_total, (0, lanes * index), (16, lanes)).astype(f32)
        mats = update(place, mine, other, mat_master, mat_first, mat_second, HALF)
    else:
        part = lax.psum_scatter(mat_grad[0], "fsdp", scatter_dimension=0, tiled=True)
        mat_total = lax.psum(part, "dp").astype(f32)
        part = lax.psum_scatter(vec_grad.astype(bf16), "fsdp", scatter_dimension=1, tiled=True)
        vec_total = lax.psum(part, "dp").astype(f32)
        sums = lax.psum(sums[:4], ("dp", "fsdp"))
        rates = row_rates(index * shard_rows + jnp.arange(shard_rows))[:, None]
        mats = adam_update(mat_master, mat_first, mat_second, mat_total, rates, WEIGHT_DECAY)
        mats += (mats[0].astype(bf16),)
    ramp_loss = sums[0] / active_count
    cls_grad = sums[1:4] / active_count
    vec_new, vec_first_new, vec_second_new = adam_update(
        vec_master, vec_first, vec_second, vec_total, VEC_RATE, 0.0
    )
    cls_new, cls_first_new, cls_second_new = adam_update(
        cls_bias, cls_first, cls_second, cls_grad, VEC_RATE, 0.0
    )
    return (
        block_out.reshape(seqs, L, D),
        input_grad,
        ramp_loss,
        *mats,
        vec_new,
        vec_first_new,
        vec_second_new,
        vec_new.astype(bf16),
        cls_new,
        cls_first_new,
        cls_second_new,
    )


def solution(mesh):
    rows = P(("dp", "fsdp"), None, None)
    each = P(("dp", "fsdp"))
    mat, vec = P("fsdp", None), P(None, "fsdp")
    paths = (mesh.shape["dp"], mesh.shape["fsdp"]) == (2, FSDP)
    return jax.shard_map(
        functools.partial(on_device, paths),
        mesh=mesh,
        in_specs=(rows, rows, each, each, each, mat, mat, mat, vec, vec, vec, P(), P(), P()),
        out_specs=(rows, rows, P(), mat, mat, mat, mat, vec, vec, vec, vec, P(), P(), P()),
        check_vma=False,
    )
```

```python
import functools
import math

import jax
import jax.numpy as jnp
from jax import lax
from jax.experimental import pallas as pl
from jax.experimental.pallas import tpu as pltpu
from jax.sharding import PartitionSpec as P

D, H, HD, FF, NCLS, L = 768, 12, 64, 3072, 3, 512
LAYER = 6
STEP = 10
BETA_ONE = 0.9
BETA_TWO = 0.999
ADAM_EPS = 1e-08
WEIGHT_DECAY = 0.01
VEC_RATE = 0.5
LN_EPS = 1e-12
MASK_FILL = -1e9
LOG2E = 1.4426950408889634
f32, bf16 = jnp.float32, jnp.bfloat16
NN = (((1,), (0,)), ((), ()))
NT = (((1,), (1,)), ((), ()))
TN = (((0,), (0,)), ((), ()))
def dot(a, b, dims=NN):
    return lax.dot_general(a, b, dims, preferred_element_type=f32)
ANY = pl.BlockSpec(memory_space=pl.ANY)
VMEM = pl.BlockSpec(memory_space=pltpu.VMEM)
HBM = pl.BlockSpec(memory_space=pltpu.HBM)
MROWS = 5 * D + 2 * FF
EARLY = 192
CHUNK = 1536
UNITS = 1536
SMEM = pl.BlockSpec(memory_space=pltpu.SMEM)
TILE = 256
R = 16


class Loads:
    def __init__(self, plan, refs, place, dst, sems, low, high):
        self.items = []
        for j, (piece, src, count, row) in enumerate(plan.spans):
            if isinstance(row, int):
                first, last = max(row, low), min(row + count, high)
                if first >= last:
                    continue
                cond = None
                source = refs[piece].at[pl.ds(src + first - row, last - first)]
                target = dst.at[pl.ds(first - low, last - first)]
            else:
                shard, at = plan.locate(row, place)
                cond = (shard * plan.rows >= low) & (shard * plan.rows < high)
                source = refs[piece].at[pl.ds(src, count)]
                target = dst.at[pl.ds(pl.multiple_of(jnp.where(cond, at - low, 0), 16), count)]
            self.items.append((cond, pltpu.make_async_copy(source, target, sems.at[j])))

    def start(self):
        for cond, copy in self.items:
            if cond is None:
                copy.start()
            else:
                pl.when(cond)(copy.start)

    def wait(self):
        for cond, copy in self.items:
            if cond is None:
                copy.wait()
            else:
                pl.when(cond)(copy.wait)


class Plan:
    def __init__(self, spans, rows, parts=(0, 0, 0)):
        self.spans, self.rows, self.parts = spans, rows, parts
        self.head_end = -(-3 * D // rows) * rows
        self.tail_start = 3 * D // rows * rows

    def locate(self, where, place):
        steps, other_x, other_core, part = where
        z, x, core, rep = (place[i] for i in range(4))
        flip = lambda bit, other: 1 - bit if other else bit
        shard = (lax.rem(z - steps + 4, 4) * 2 + flip(x, other_x)) * 2 + flip(core, other_core)
        a, c, e = self.parts
        base = {
            "all": 0,
            "a": 0,
            "c_mine": a + rep * c,
            "c_other": a + (1 - rep) * c,
            "e": a + 2 * c,
            "e_late": a + 2 * c + EARLY,
            "e_mine": a + 2 * c + rep * e,
            "e_other": a + 2 * c + (1 - rep) * e,
        }[part]
        return shard, shard * self.rows + base


class Layout:
    def __init__(self, rows, half):
        self.rows, self.half = rows, half
        self.shapes = [jax.ShapeDtypeStruct((2 * rows, D), bf16)] * 8 if half else [jax.ShapeDtypeStruct((MROWS, D), bf16)]

    def write(self, place, staged, low, targets, sem, first, count):
        def start(target, at, rows, row):
            pltpu.make_async_copy(staged.at[pl.ds(at - low, rows)], target.at[pl.ds(row, rows)], sem).start()

        if not self.half:
            start(targets[0], first, count, first)
            return
        z, x, core, rep = (place[i] for i in range(4))
        rows, half = self.rows, self.half
        for shard in range(first // rows, -(-(first + count) // rows)):
            far_x, far_core = jnp.abs(x - shard // 2 % 2), jnp.abs(core - shard % 2)
            group = far_core * 4 + lax.rem(z - shard // 4 + 4, 4)
            runs = (
                (0, half, rep * 2 * half + far_x * half),
                (half, half, (1 - rep) * 2 * half + far_x * half),
                (2 * half, rows - 2 * half, 4 * half + (1 - far_x) * (rows - 2 * half)),
            )

            def put(target, shard=shard, runs=runs):
                for inner, size, row in runs:
                    begin = max(first, shard * rows + inner)
                    end = min(first + count, shard * rows + inner + size)
                    if begin < end:
                        start(target, begin, end - begin, pl.multiple_of(row + begin - shard * rows - inner, 16))

            for index, target in enumerate(targets):
                pl.when(group == index)(functools.partial(put, target))

    def wait(self, staged, low, targets, sem, first, count):
        rows = staged.at[pl.ds(first - low, count)]
        pltpu.make_async_copy(rows, rows, sem).wait()


def attn_fwd_kernel(plan, n, place, lens, x_ref, vec_ref, *refs):
    pieces = refs[:n]; qkv_ref, ctx_ref, st_ref, w, sems = refs[n:]
    s = pl.program_id(0)
    @pl.when(s == 0)
    def _():
        ld = Loads(plan, pieces, place, w, sems, 0, plan.head_end)
        ld.start(); ld.wait()
    x = x_ref[0]
    for i, b in ((0, 0), (1, None), (2, 1)):
        r = dot(x, w[i * D:(i + 1) * D])
        if b is not None: r = r + vec_ref[b:b + 1]
        qkv_ref[0, :, i * D:(i + 1) * D] = r.astype(bf16)
    length = lens[s]
    lane = lax.broadcasted_iota(jnp.int32, (L, 128), 1)
    low = lane < HD
    valid = lax.broadcasted_iota(jnp.int32, (1, L), 1) < length
    ones = jnp.ones((L, 128), bf16)
    stats = jnp.zeros((L, 128), f32)
    scale = LOG2E * HD ** -0.5
    for p in range(H // 2):
        q2 = qkv_ref[0, :, p * 128:(p + 1) * 128]
        k2 = qkv_ref[0, :, D + p * 128:D + (p + 1) * 128]
        v2 = qkv_ref[0, :, 2 * D + p * 128:2 * D + (p + 1) * 128]
        va = jnp.concatenate([v2, ones], axis=1)
        outs = []
        for h in range(2):
            qm = jnp.where(low if h == 0 else ~low, q2, jnp.zeros_like(q2))
            sc = jnp.where(valid, dot(qm, k2, NT) * scale, MASK_FILL)
            top = jnp.max(sc, axis=1, keepdims=True)
            e = jnp.exp2(sc - top).astype(bf16)
            o = dot(e, va)
            tot = o[:, 128:]
            outs.append(o[:, :128] / tot)
            stats = jnp.where(lane == 2 * p + h, top + jnp.log2(tot), stats)
        ctx_ref[0, :, p * 128:(p + 1) * 128] = jnp.where(low, outs[0], outs[1]).astype(bf16)
    st_ref[0] = stats.T

def attn_fwd(plan, pieces, place, lengths, tokens, vec):
    n = len(pieces); S = tokens.shape[0]
    return pl.pallas_call(
        functools.partial(attn_fwd_kernel, plan, n), grid=(S,), name="attn_fwd",
        in_specs=[SMEM, SMEM, pl.BlockSpec((1, L, D), lambda s: (s, 0, 0)), pl.BlockSpec((16, D), lambda s: (0, 0))] + [HBM] * n,
        out_specs=[pl.BlockSpec((1, L, 3 * D), lambda s: (s, 0, 0)), pl.BlockSpec((1, L, D), lambda s: (s, 0, 0)), pl.BlockSpec((1, 128, L), lambda s: (s, 0, 0))],
        out_shape=[jax.ShapeDtypeStruct((S, L, 3 * D), bf16), jax.ShapeDtypeStruct((S, L, D), bf16), jax.ShapeDtypeStruct((S, 128, L), f32)],
        scratch_shapes=[pltpu.VMEM((plan.head_end, D), bf16), pltpu.SemaphoreType.DMA((len(plan.spans),))],
        compiler_params=pltpu.CompilerParams(vmem_limit_bytes=50 << 20),
        cost_estimate=pl.CostEstimate(flops=8 * 10 ** 9, bytes_accessed=14 * 10 ** 6, transcendentals=6 * 10 ** 6),
    )(place, lengths, tokens, vec, *pieces)

def norm(h):
    mu = jnp.mean(h, axis=1, keepdims=True)
    c = h - mu
    r = lax.rsqrt(jnp.mean(c * c, axis=1, keepdims=True) + LN_EPS)
    return c * r, r

def norm_back(g, xh, r, gain):
    a = g * gain
    return r * (a - jnp.mean(a, axis=1, keepdims=True) - xh * jnp.mean(a * xh, axis=1, keepdims=True))

def gelu_both(u):
    phi = 0.5 + 0.5 * lax.erf(u * 2**-0.5)
    bell = jnp.exp2(u * u * (-0.5 * LOG2E))
    return u * phi, phi + (u * bell) * (2 * math.pi) ** -0.5


def ffn_kernel(plan, layout, n, tiles, low, place, labels, exits, count, cls, x_ref, c_ref, og_ref, vec_ref, *refs):
    m = n + 5 + len(layout.shapes)
    pieces, gw_refs = refs[:n], refs[n + 5:m]
    out_ref, dh1_ref, dc_ref, vg_ref, sc_ref = refs[n:n + 5]
    w, sems, g_s, du_s, n1_s, df_s, da_s, cc_s, gp_s, dy_s, e_s, z_s, osem = refs[m:]
    i = pl.program_id(0)
    ld = Loads(plan, pieces, place, w, sems, low, MROWS)
    @pl.when(i == 0)
    def _():
        ld.start()
        vg_ref[...] = jnp.zeros_like(vg_ref); sc_ref[...] = jnp.zeros_like(sc_ref)
        ld.wait()
    wo, wp, w1, w2 = 3 * D - low, 4 * D - low, 5 * D - low, 5 * D + FF - low
    vrow = lambda r: vec_ref[r:r + 1]
    rows = pl.ds(pl.multiple_of(i * TILE, TILE), TILE)
    c = c_ref[...]
    cc_s[rows] = c
    h1 = x_ref[...].astype(f32) + (dot(c, w[wo:wo + D]) + vrow(2))
    xh1, r1 = norm(h1)
    n1 = xh1 * vrow(3) + vrow(4)
    n1b = n1.astype(bf16)
    n1_s[rows] = n1b
    f = None
    for j in range(0, FF, UNITS):
        bias = jnp.concatenate([vrow(9 + i) for i in range(j // D, (j + UNITS) // D)], axis=1)
        g, gp = gelu_both(dot(n1b, w[w1 + j:w1 + j + UNITS], NT) + bias)
        gb = g.astype(bf16)
        g_s[rows, j:j + UNITS] = gb
        gp_s[:, j:j + UNITS] = gp
        part = dot(gb, w[w2 + j:w2 + j + UNITS])
        f = part if f is None else f + part
    xh2, r2 = norm(n1 + (f + vrow(5)))
    yb = (xh2 * vrow(6) + vrow(7)).astype(bf16)
    out_ref[...] = yb
    dy_s[...] = og_ref[...].astype(f32)
    per = L // TILE
    @pl.when(lax.rem(i, per) == 0)
    def _():
        s = i // per
        head = lax.broadcasted_iota(jnp.int32, (R, 1), 0) == 0
        act = jnp.where(head, jnp.where(exits[s] >= LAYER, 1.0, 0.0), 0.0)
        e8 = jnp.where(head, yb[:R].astype(f32), 0.0).astype(bf16)
        pool = jnp.tanh(dot(e8, w[wp:wp + D]) + vrow(8))
        pb = pool.astype(bf16).astype(f32)
        lg = [jnp.sum(pb * vrow(13 + k), axis=1, keepdims=True) + cls[k] for k in range(NCLS)]
        top = jnp.maximum(jnp.maximum(lg[0], lg[1]), lg[2])
        lse = top + jnp.log(jnp.exp(lg[0] - top) + jnp.exp(lg[1] - top) + jnp.exp(lg[2] - top))
        hot = [jnp.where(labels[s] == k, 1.0, 0.0) for k in range(NCLS)]
        ce = act * (lse - (lg[0] * hot[0] + lg[1] * hot[1] + lg[2] * hot[2]))
        err = [act * (jnp.exp(lg[k] - lse) - hot[k]) for k in range(NCLS)]
        lane = lax.broadcasted_iota(jnp.int32, (R, 128), 1)
        got = jnp.where(lane == 0, ce, 0.0)
        for k in range(NCLS): got = jnp.where(lane == 1 + k, err[k], got)
        sc_ref[...] += got
        dl = [(err[k] / count[0]).astype(bf16).astype(f32) for k in range(NCLS)]
        gpool = dl[0] * vrow(13) + dl[1] * vrow(14) + dl[2] * vrow(15)
        dz = (gpool * (1.0 - pool * pool)).astype(bf16)
        srow = pl.ds(pl.multiple_of(s * R, R), R)
        e_s[srow] = e8; z_s[srow] = dz
        vg_ref[8:9] += jnp.sum(dz.astype(f32), axis=0, keepdims=True)
        for k in range(NCLS): vg_ref[13 + k:14 + k] += jnp.sum(dl[k] * pb, axis=0, keepdims=True)
        dy_s[0:R] += dot(dz, w[wp:wp + D], NT)
    dy = dy_s[...]
    def vsum(r, v): vg_ref[r:r + 1] += jnp.sum(v, axis=0, keepdims=True)
    vsum(6, dy * xh2); vsum(7, dy)
    dh2 = norm_back(dy, xh2, r2, vrow(6))
    dfb = dh2.astype(bf16)
    df_s[rows] = dfb
    vsum(5, dfb.astype(f32))
    dn1 = dh2
    for j in range(0, FF, UNITS):
        du = (dot(dfb, w[w2 + j:w2 + j + UNITS], NT) * gp_s[:, j:j + UNITS]).astype(bf16)
        du_s[rows, j:j + UNITS] = du
        for part_at in range(0, UNITS, D):
            vsum(9 + (part_at + j) // D, du[:, part_at:part_at + D].astype(f32))
        dn1 = dn1 + dot(du, w[w1 + j:w1 + j + UNITS])
    vsum(3, dn1 * xh1); vsum(4, dn1)
    dh1 = norm_back(dn1, xh1, r1, vrow(3))
    dh1_ref[...] = dh1
    dab = dh1.astype(bf16)
    da_s[rows] = dab
    vsum(2, dab.astype(f32))
    dc_ref[...] = dot(dab, w[wo:wo + D], NT).astype(bf16)
    @pl.when(i == tiles - 1)
    def _():
        for lhs, rhs, width, base in ((e_s, z_s, D, 4 * D), (cc_s, da_s, D, 3 * D), (du_s, n1_s, FF, 5 * D), (g_s, df_s, FF, 5 * D + FF)):

            size = min(width, CHUNK)

            def step(r, carry, lhs=lhs, rhs=rhs, base=base, size=size):
                at = pl.multiple_of(r * size, size)
                w[pl.ds(pl.multiple_of(base - low + at, 16), size)] = dot(lhs[:, pl.ds(at, size)], rhs[...], TN).astype(bf16)
                return carry

            lax.fori_loop(0, width // size, step, 0)
            layout.write(place, w, low, gw_refs, osem.at[0], base, width)
        layout.wait(w, low, gw_refs, osem.at[0], 3 * D, MROWS - 3 * D)

def ffn(plan, layout, pieces, place, labels, exits, count, cls, x, ctx, og, vec):
    n = len(pieces); T = x.shape[0]; tiles = T // TILE; low = plan.tail_start
    tok = lambda dt: pl.BlockSpec((TILE, D), lambda i: (i, 0))
    return pl.pallas_call(
        functools.partial(ffn_kernel, plan, layout, n, tiles, low), grid=(tiles,), name="ffn",
        in_specs=[SMEM] * 5 + [tok(0)] * 3 + [pl.BlockSpec((16, D), lambda i: (0, 0))] + [HBM] * n,
        out_specs=[tok(0), tok(0), tok(0), pl.BlockSpec((16, D), lambda i: (0, 0)), pl.BlockSpec((R, 128), lambda i: (0, 0))] + [ANY] * len(layout.shapes),
        out_shape=[jax.ShapeDtypeStruct((T, D), bf16), jax.ShapeDtypeStruct((T, D), f32), jax.ShapeDtypeStruct((T, D), bf16), jax.ShapeDtypeStruct((16, D), f32), jax.ShapeDtypeStruct((R, 128), f32)] + layout.shapes,
        scratch_shapes=[pltpu.VMEM((MROWS - low, D), bf16), pltpu.SemaphoreType.DMA((len(plan.spans),)),
            pltpu.VMEM((T, FF), bf16), pltpu.VMEM((T, FF), bf16), pltpu.VMEM((T, D), bf16), pltpu.VMEM((T, D), bf16), pltpu.VMEM((T, D), bf16), pltpu.VMEM((T, D), bf16),
            pltpu.VMEM((TILE, FF), f32), pltpu.VMEM((TILE, D), f32), pltpu.VMEM((R * (T // L), D), bf16), pltpu.VMEM((R * (T // L), D), bf16),
            pltpu.SemaphoreType.DMA((1,))],
        compiler_params=pltpu.CompilerParams(vmem_limit_bytes=60 << 20),
        cost_estimate=pl.CostEstimate(flops=33 * 10 ** 9, bytes_accessed=40 * 10 ** 6, transcendentals=6 * 10 ** 6),
    )(place, labels, exits, count, cls, x, ctx, og, vec, *pieces)

def attn_bwd_kernel(plan, layout, n, S, place, lens, x_ref, qkv_ref, dc_ref, c_ref, st_ref, dh1_ref, *refs):
    m = len(layout.shapes)
    pieces = refs[:n]
    dx_ref, vg_ref = refs[n + m:n + m + 2]
    gw_refs = refs[n + m + 2:n + 2 * m + 2]
    w, sems, d_s, x_s, osem = refs[n + 2 * m + 2:]
    s = pl.program_id(0)
    ld = Loads(plan, pieces, place, w, sems, 0, plan.head_end)
    @pl.when(s == 0)
    def _():
        ld.start()
        vg_ref[...] = jnp.zeros_like(vg_ref)
    rows = pl.ds(pl.multiple_of(s * L, L), L)
    x_s[rows] = x_ref[0]
    length = lens[s]
    low = lax.broadcasted_iota(jnp.int32, (L, 128), 1) < HD
    zero = jnp.zeros((L, 128), bf16)
    apart = lambda v: jnp.concatenate([jnp.where(low, v, zero), jnp.where(low, zero, v)], axis=0)
    join = lambda v: jnp.where(low, v[:L], v[L:])
    valid = lax.broadcasted_iota(jnp.int32, (L, 1), 0) < length
    scale = LOG2E * HD ** -0.5
    at = lambda i, p: slice(i * D + p * 128, i * D + (p + 1) * 128)

    def scores(p):
        q2, k2, v2 = (qkv_ref[0, :, at(i, p)] for i in range(3))
        ks, dc2 = apart(k2), dc_ref[0, :, at(0, p)]
        return ks, q2, dc2, dot(ks, q2, NT), dot(apart(v2), dc2, NT)

    ahead = scores(0)
    for p in range(H // 2):
        ks, q2, dc2, score, dprob = ahead
        if p + 1 < H // 2:
            ahead = scores(p + 1)
        prod = (dc2.astype(f32) * c_ref[0, :, at(0, p)].astype(f32)).T
        probs, dscores = [], []
        for h in range(2):
            delta = jnp.sum(prod[h * HD:(h + 1) * HD], axis=0, keepdims=True)
            rows_h = slice(h * L, (h + 1) * L)
            st = jnp.where(valid, score[rows_h] * scale, MASK_FILL)
            pt = jnp.exp2(st - st_ref[0, 2 * p + h:2 * p + h + 1, :])
            probs.append(pt.astype(bf16))
            dscores.append((pt * (dprob[rows_h] - delta)).astype(bf16))
        dst = jnp.concatenate(dscores, axis=0)
        d_s[rows, at(0, p)] = (dot(dst, ks, TN) * HD ** -0.5).astype(bf16)
        d_s[rows, at(1, p)] = (join(dot(dst, q2)) * HD ** -0.5).astype(bf16)
        d_s[rows, at(2, p)] = join(dot(jnp.concatenate(probs, axis=0), dc2)).astype(bf16)
    @pl.when(s == 0)
    def _(): ld.wait()
    dq, dk, dv = (d_s[rows, i * D:(i + 1) * D] for i in range(3))
    dx_ref[0] = (dh1_ref[0] + dot(dq, w[0:D], NT) + dot(dk, w[D:2 * D], NT) + dot(dv, w[2 * D:3 * D], NT)).astype(bf16)
    vg_ref[0:1] += jnp.sum(dq.astype(f32), axis=0, keepdims=True)
    vg_ref[1:2] += jnp.sum(dv.astype(f32), axis=0, keepdims=True)
    @pl.when(s == S - 1)
    def _():
        for i in range(3):
            w[i * D:(i + 1) * D] = dot(x_s[...], d_s[:, i * D:(i + 1) * D], TN).astype(bf16)
            layout.write(place, w, 0, gw_refs, osem.at[0], i * D, D)
        layout.wait(w, 0, gw_refs, osem.at[0], 0, 3 * D)

def attn_bwd(plan, layout, pieces, place, lengths, tokens, qkv, dc, ctx, st, dh1, gw):
    n, m, S = len(pieces), len(gw), tokens.shape[0]
    seq = lambda *sh: pl.BlockSpec((1,) + sh, lambda s: (s, 0, 0))
    return pl.pallas_call(
        functools.partial(attn_bwd_kernel, plan, layout, n, S), grid=(S,), name="attn_bwd",
        in_specs=[SMEM, SMEM, seq(L, D), seq(L, 3 * D), seq(L, D), seq(L, D), seq(128, L), seq(L, D)] + [HBM] * n + [ANY] * m,
        out_specs=[seq(L, D), pl.BlockSpec((8, D), lambda s: (0, 0))] + [ANY] * m,
        out_shape=[jax.ShapeDtypeStruct((S, L, D), bf16), jax.ShapeDtypeStruct((8, D), f32)] + layout.shapes,
        input_output_aliases={8 + n + i: 2 + i for i in range(m)},
        scratch_shapes=[pltpu.VMEM((plan.head_end, D), bf16), pltpu.SemaphoreType.DMA((len(plan.spans),)), pltpu.VMEM((S * L, 3 * D), bf16), pltpu.VMEM((S * L, D), bf16), pltpu.SemaphoreType.DMA((1,))],
        compiler_params=pltpu.CompilerParams(vmem_limit_bytes=56 << 20),
        cost_estimate=pl.CostEstimate(flops=16 * 10 ** 9, bytes_accessed=24 * 10 ** 6, transcendentals=6 * 10 ** 6),
    )(place, lengths, tokens, qkv, dc, ctx, st, dh1, *pieces, *gw)


FSDP = 16


WAYS = {
    "x": ("fsdp", tuple((i, i ^ 2) for i in range(FSDP))),
    "y": ("dp", ((0, 1), (1, 0))),
    "z": ("fsdp", tuple((i, (i + 4) % FSDP) for i in range(FSDP))),
    "core": ("fsdp", tuple((i, i ^ 1) for i in range(FSDP))),
}
PARTS = (80, 128, 144)
HALF = 160
BLOCKS = 3


def hold(value, *others):
    return lax.optimization_barrier((value, *others))[0] if others else value


def send(way, *values):
    return lax.ppermute(values[0] if len(values) == 1 else jnp.concatenate(values), *WAYS[way])


def position():
    index = lax.axis_index("fsdp")
    return index // 4, index // 2 % 2, index % 2, lax.axis_index("dp")


def gather(shard, small):
    a, c, e = PARTS
    rows, rep = shard.shape[0], lax.axis_index("dp")
    cut = lax.dynamic_slice_in_dim
    all_a, all_e = shard[:a], shard[a + 2 * c :]
    my_c, my_e = cut(shard, a + rep * c, c), cut(shard, a + 2 * c + rep * e, e)
    late = 2 * e - EARLY
    zc, ze = (lambda k: z[k][:c]), (lambda k: z[k][c : c + e])
    z, za = {}, {}
    z[1] = send("z", my_c, my_e, small)
    x1 = send("x", all_a, my_c, all_e[:EARLY])
    z[2] = send("z", z[1])
    x2 = send("x", all_e[EARLY:], zc(1))
    y2 = send("y", x1[a : a + c], ze(1))
    za[1] = send("z", all_a, x1[:a])
    x3 = send("x", zc(2), ze(1), y2[c:])
    y3 = send("y", zc(1), x2[late:], ze(2))
    z[3] = send("z", hold(z[2], x2))
    za[2] = send("z", hold(za[1], y2, x2))
    small = small + z[1][c + e :] + z[2][c + e :] + z[3][c + e :]
    x4 = send("x", zc(3), ze(2), y3[2 * c :], small)
    y4 = send("y", zc(2), x3[:c], ze(3))
    za[3] = send("z", hold(za[2], y3, x3))
    small = small + x4[c + 2 * e :]
    x5 = send("x", ze(3), y4[2 * c :])
    y5 = send("y", zc(3), x4[:c], small)
    small = small + y5[2 * c :]
    za = {1: hold(za[1], x3, y3), 2: hold(za[2], x4, y4), 3: hold(za[3], x5, y5)}
    small = small + send("core", small)
    held = [(shard, ((0, rows, 0, 0, "all"),))]
    for k in (1, 2, 3):
        held.append((z[k], ((0, c, k, 0, "c_mine"), (c, e, k, 0, "e_mine"))))
        held.append((za[k], ((0, a, k, 0, "a"), (a, a, k, 1, "a"))))
    held.append((x1, ((0, a, 0, 1, "a"), (a, c, 0, 1, "c_mine"), (a + c, EARLY, 0, 1, "e"))))
    held.append((x2, ((0, late, 0, 1, "e_late"), (late, c, 1, 1, "c_mine"))))
    held.append((y2, ((0, c, 0, 1, "c_other"), (c, e, 1, 0, "e_other"))))
    for k, x_got, y_got in ((2, x3, y3), (3, x4, y4)):
        held.append((x_got, ((0, c, k, 1, "c_mine"), (c, e, k - 1, 1, "e_mine"), (c + e, e, k - 1, 1, "e_other"))))
        held.append((y_got, ((0, c, k - 1, 0, "c_other"), (c, c, k - 1, 1, "c_other"), (2 * c, e, k, 0, "e_other"))))
    held.append((x5, ((0, e, 3, 1, "e_mine"), (e, e, 3, 1, "e_other"))))
    held.append((y5, ((0, c, 3, 0, "c_other"), (c, c, 3, 1, "c_other"))))
    pieces, plan = [], Plan([], rows, PARTS)
    for value, parts in held:
        for other_core, piece in ((0, value), (1, send("core", value))):
            for start, count, steps, other_x, part in parts:
                plan.spans.append((len(pieces), start, count, (steps, other_x, other_core, part)))
            pieces.append(piece)
    return pieces, plan, small


def add_low(a, b):
    return (a.astype(f32) + b.astype(f32)).astype(bf16)


def scatter_sum(grads, small, sums, half):
    rows = grads[0].shape[0] // 2
    c, e = half, rows // 2 - half
    rep = lax.axis_index("dp")
    cut = lax.dynamic_slice_in_dim
    links = {"x": [], "y": [], "z": []}

    def link(name, *values):
        done = links[name]
        first = hold(values[0], *done[-2:-1])
        done.append(send(name, first, *values[1:]))
        return done[-1]

    def packed():
        high = sums.astype(bf16)
        low = (sums - high.astype(f32)).astype(bf16)
        return jnp.concatenate([small, jnp.stack([high, low] + [jnp.zeros_like(high)] * 6)])

    def added(others):
        total, total_sums = small.astype(f32), sums
        for other in others:
            total = total + other[:16].astype(f32)
            total_sums = total_sums + (other[16].astype(f32) + other[17].astype(f32))
        return total.astype(bf16), total_sums

    small, sums = added([send("core", packed())])
    riders = []
    ring_c = ring_e = None
    for k in (1, 2, 3, 0):
        keep, got = grads[k], send("core", grads[4 + k])
        part = lambda first, count: add_low(keep[first : first + count], got[first : first + count])
        along = (lambda: (packed(),)) if k == 1 else tuple
        yc = link("y", part(2 * c, 2 * c), *along())
        xe = link("x", part(4 * c, 2 * e))
        both_c = add_low(part(0, 2 * c), yc[: 2 * c])
        own_e = add_low(part(4 * c + 2 * e, 2 * e), xe)
        if k == 1:
            small, sums = added([yc[2 * c :]])
        xc = link("x", both_c[c:], *along())
        if k == 1:
            small, sums = added([xc[c:]])
            riders.append(packed())
        ye = link("y", cut(own_e, (1 - rep) * e, e))
        sum_c = both_c[:c].astype(f32) + xc[:c].astype(f32)
        sum_e = cut(own_e, rep * e, e).astype(f32) + ye.astype(f32)
        if ring_c is not None:
            sum_c, sum_e = sum_c + ring_c.astype(f32), sum_e + ring_e[:e].astype(f32)
        sum_c, sum_e = sum_c.astype(bf16), sum_e.astype(bf16)
        if k:
            ring_c, ring_e = link("z", sum_c), link("z", sum_e, riders[-1])
            riders.append(ring_e[e:])
    small, sums = added(riders[1:])
    mine = jnp.concatenate([sum_c, sum_e])
    return mine, send("y", mine), small, sums


def stage_kernel(after, *refs):
    copies = [pltpu.make_async_copy(refs[i], refs[3 + i], refs[6].at[i]) for i in range(3)]
    for copy in copies:
        copy.start()
    for copy in copies:
        copy.wait()


def update_kernel(half, place, mine, other, master, first, second, *refs):
    targets, (grad, *values), sems = refs[:4], refs[4:9], refs[9]
    c, rows = half, grad.shape[0]
    e, count = rows // 2 - half, rows // BLOCKS
    rep = place[3]
    for start, size, at in ((0, c, 0), (c, e, 2 * c)):
        ours, theirs = mine[start : start + size].astype(f32), other[start : start + size].astype(f32)
        grad[at : at + size] = jnp.where(rep == 0, ours, theirs)
        grad[at + size : at + 2 * size] = jnp.where(rep == 0, theirs, ours)
    shard = (place[0] * 2 + place[1]) * 2 + place[2]
    copies = []
    for block in range(BLOCKS):
        at = pl.ds(block * count, count)
        row = shard * rows + block * count + lax.broadcasted_iota(jnp.int32, (count, 1), 0)
        results = adam_update(master[at], first[at], second[at], grad[at], row_rates(row), WEIGHT_DECAY)
        for i, result in enumerate(results + (results[0].astype(bf16),)):
            values[i][at] = result
            copies.append(pltpu.make_async_copy(values[i].at[at], targets[i].at[at], sems.at[block * 4 + i]))
            copies[-1].start()
    for copy in copies:
        copy.wait()


def update(place, mine, other, master, first, second, half):
    rows = master.shape[0]
    staged = pl.pallas_call(
        stage_kernel,
        name="stage",
        in_specs=[ANY] + [HBM] * 3,
        out_specs=[VMEM] * 3,
        out_shape=[pltpu.VMEM((rows, D), f32)] * 3,
        scratch_shapes=[pltpu.SemaphoreType.DMA((3,))],
        compiler_params=pltpu.CompilerParams(vmem_limit_bytes=4 << 20),
        cost_estimate=pl.CostEstimate(flops=10**6, bytes_accessed=6 * 10**6, transcendentals=0),
    )(mine, master, first, second)
    types = (f32, f32, f32, bf16)
    return pl.pallas_call(
        functools.partial(update_kernel, half),
        name="update",
        in_specs=[SMEM] + [VMEM] * 5,
        out_specs=[HBM] * 4,
        out_shape=[jax.ShapeDtypeStruct((rows, D), dtype) for dtype in types],
        scratch_shapes=[pltpu.VMEM((rows, D), dtype) for dtype in (f32, *types)] + [pltpu.SemaphoreType.DMA((4 * BLOCKS,))],
        compiler_params=pltpu.CompilerParams(vmem_limit_bytes=24 << 20),
        cost_estimate=pl.CostEstimate(flops=10**7, bytes_accessed=7 * 10**6, transcendentals=10**6),
    )(place, mine, other, *staged)


def row_rates(row_index):
    base_rate = D ** (-0.5)
    return jnp.where(
        (row_index >= 3 * D) & (row_index < 4 * D),
        8.0 * base_rate,
        jnp.where(row_index >= 5 * D + FF, 1.5 * FF ** (-0.5), base_rate),
    )


def adam_update(master, first_mom, second_mom, grad_in, rate, decay):
    first_new = BETA_ONE * first_mom + (1.0 - BETA_ONE) * grad_in
    second_new = BETA_TWO * second_mom + (1.0 - BETA_TWO) * grad_in * grad_in
    fix_one = 1.0 - BETA_ONE**STEP
    fix_two = 1.0 - BETA_TWO**STEP
    direction = first_new / fix_one / (jnp.sqrt(second_new / fix_two) + ADAM_EPS)
    master_new = master - rate * (direction + decay * master)
    return (master_new, first_new, second_new)


def on_device(
    paths,
    tokens,
    out_grad,
    lengths,
    labels,
    exit_layers,
    mat_master,
    mat_first,
    mat_second,
    vec_master,
    vec_first,
    vec_second,
    cls_bias,
    cls_first,
    cls_second,
):
    seqs, toks = tokens.shape[0], tokens.shape[0] * L
    shard_rows, lanes = mat_master.shape[0], vec_master.shape[1]
    index = lax.axis_index("fsdp")
    place = jnp.stack(position()).astype(jnp.int32)
    active = jnp.sum((exit_layers >= LAYER).astype(f32))
    mat_low, vec_low = mat_master.astype(bf16), vec_master.astype(bf16)
    if paths:
        placed = lax.dynamic_update_slice(jnp.zeros((16, D), bf16), vec_low, (0, lanes * index))
        placed = jnp.where(lax.axis_index("dp") == 0, placed, jnp.zeros_like(placed))
        layout = Layout(shard_rows, HALF)
        pieces, plan, small = gather(mat_low, jnp.concatenate([placed, jnp.full((8, D), active).astype(bf16)]))
        vectors, active_count = small[:16].astype(f32), small[16, 0].astype(f32)
    else:
        pieces = [lax.all_gather(mat_low, "fsdp", axis=0, tiled=True)]
        plan, layout = Plan([(0, 0, MROWS, 0)], 3 * D), Layout(shard_rows, 0)
        vectors = lax.all_gather(vec_low, "fsdp", axis=1, tiled=True).astype(f32)
        active_count = lax.psum(active, ("dp", "fsdp"))
    qkv, context, stats = attn_fwd(plan, pieces, place, lengths, tokens, vectors)
    block_out, grad_attn, grad_ctx, vec_grad, sums, *mat_grad = ffn(
        plan,
        layout,
        pieces,
        place,
        labels,
        exit_layers,
        active_count.reshape(1),
        cls_bias,
        tokens.reshape(toks, D),
        context.reshape(toks, D),
        out_grad.reshape(toks, D),
        vectors,
    )
    input_grad, head_grad, *mat_grad = attn_bwd(
        plan,
        layout,
        pieces,
        place,
        lengths,
        tokens,
        qkv,
        grad_ctx.reshape(seqs, L, D),
        context,
        stats,
        grad_attn.reshape(seqs, L, D),
        mat_grad,
    )
    vec_grad = jnp.concatenate([head_grad[:2], vec_grad[2:]])
    sums = jnp.sum(sums, axis=0)
    if paths:
        sums = jnp.pad(sums, (0, D - 128))
        mine, other, vec_total, sums = scatter_sum(mat_grad, vec_grad.astype(bf16), sums, HALF)
        vec_total = lax.dynamic_slice(vec_total, (0, lanes * index), (16, lanes)).astype(f32)
        mats = update(place, mine, other, mat_master, mat_first, mat_second, HALF)
    else:
        part = lax.psum_scatter(mat_grad[0], "fsdp", scatter_dimension=0, tiled=True)
        mat_total = lax.psum(part, "dp").astype(f32)
        part = lax.psum_scatter(vec_grad.astype(bf16), "fsdp", scatter_dimension=1, tiled=True)
        vec_total = lax.psum(part, "dp").astype(f32)
        sums = lax.psum(sums[:4], ("dp", "fsdp"))
        rates = row_rates(index * shard_rows + jnp.arange(shard_rows))[:, None]
        mats = adam_update(mat_master, mat_first, mat_second, mat_total, rates, WEIGHT_DECAY)
        mats += (mats[0].astype(bf16),)
    ramp_loss = sums[0] / active_count
    cls_grad = sums[1:4] / active_count
    vec_new, vec_first_new, vec_second_new = adam_update(
        vec_master, vec_first, vec_second, vec_total, VEC_RATE, 0.0
    )
    cls_new, cls_first_new, cls_second_new = adam_update(
        cls_bias, cls_first, cls_second, cls_grad, VEC_RATE, 0.0
    )
    return (
        block_out.reshape(seqs, L, D),
        input_grad,
        ramp_loss,
        *mats,
        vec_new,
        vec_first_new,
        vec_second_new,
        vec_new.astype(bf16),
        cls_new,
        cls_first_new,
        cls_second_new,
    )


def solution(mesh):
    rows = P(("dp", "fsdp"), None, None)
    each = P(("dp", "fsdp"))
    mat, vec = P("fsdp", None), P(None, "fsdp")
    paths = (mesh.shape["dp"], mesh.shape["fsdp"]) == (2, FSDP)
    return jax.shard_map(
        functools.partial(on_device, paths),
        mesh=mesh,
        in_specs=(rows, rows, each, each, each, mat, mat, mat, vec, vec, vec, P(), P(), P()),
        out_specs=(rows, rows, P(), mat, mat, mat, mat, vec, vec, vec, vec, P(), P(), P()),
        check_vma=False,
    )
```
